32 devices in a mesh: aa: 8 (over z, x), ba: 4 (over y, core).
Axes of the slice: x: 2, y: 2, z: 4, core: 2. Of those that a mesh axis runs over, the one named last changes fastest.
Arguments:
- prev_vector: float32 [4608, 6144], P('aa', 'ba'), may hold values from -6 to 6
- this_vector: float32 [4608, 6144], P('aa', 'ba'), may hold values from -6 to 6
- diagonal: float32 [4608, 6144], P('aa', 'ba'), may hold values from -0.5 to 0.5
- alpha_blocks: bfloat16 [36, 2, 128, 128], replicated, may hold values from -0.21875 to 0.21875
- alpha_classes: int32 [8], replicated, may hold values from 1 to 8, 36 in all
- alpha_offsets: int32 [36, 2], replicated, may hold values from 0 to 7
- alpha_mask: int32 [36, 2], replicated, may hold values 0 or 1
- beta_blocks: bfloat16 [48, 2, 128, 128], replicated, may hold values from -0.21875 to 0.21875
- beta_classes: int32 [8], replicated, may hold values from 1 to 10, 48 in all
- beta_offsets: int32 [48, 2], replicated, may hold values from 0 to 9
- beta_mask: int32 [48, 2], replicated, may hold values 0 or 1
Outputs:
- next_vector: float32 [4608, 6144], P('aa', 'ba')
- after_vector: float32 [4608, 6144], P('aa', 'ba')
The draws below stay inside these ranges and needn't reach their ends.
Inputs may be any that keep to these rules, and one draw needn't show every extreme that they name: `alpha_classes`: alpha strings are ordered by class; the class sizes sum to 36 blocks and one class has exactly 8 blocks. `beta_classes`: beta strings are ordered by class; the class sizes sum to 48 blocks and one class has exactly 10 blocks.
All inputs are finite; a program needn't handle non-finite values.
Results may differ from the reference program's by a relative error of at most 0.0065.
Values may be sent and summed in bfloat16 or wider, within the bound.
No kernel may reach another device: no remote copies, remote signals or barrier semaphores. Data moves between devices by JAX's collectives and lax.ppermute only.
A program may use at most 128 MiB of HBM per device.

```python
import math
import jax
import jax.numpy as jnp
import numpy as np
from jax import lax

NA = 4608
NB = 6144
BLK = 128
NCLS = 8
A_MOST = 8
B_MOST = 10
SLOTS = 2
STEPS = 2
NBLK_A = 36
NBLK_B = 48


def place_ends(values, key, low, largest):
    spot = [jax.random.randint(jax.random.fold_in(key, axis), (), 0, length) for axis, length in enumerate(values.shape)]
    widest = values.shape.index(max(values.shape))
    neighbour = spot[:widest] + [(spot[widest] + 1) % values.shape[widest]] + spot[widest + 1:]
    return values.at[tuple(spot)].set(low).at[tuple(neighbour)].set(largest)


def level_of(own_key, extent, split, low, top_value):
    def one(axis_at, parts):
        draws = jax.random.uniform(jax.random.fold_in(jax.random.fold_in(own_key, 6), axis_at), (parts,), jnp.float32, low / len(split), top_value / len(split))
        return jnp.repeat(jnp.exp(draws), extent[axis_at] // parts).reshape((-1,) + (1,) * (len(extent) - axis_at - 1))

    level = one(*split[0])
    for cut in split[1:]:
        level = level * one(*cut)
    return level


def length_profile(count, total, bound, skew):
    weights = [(1 << 20) // math.isqrt(rank ** skew) + 1 for rank in range(2, count + 1)]
    spare, given = total - bound - (count - 1), [1] * (count - 1)
    while spare > 0:
        free = [i for i in range(count - 1) if given[i] < bound]
        whole, remaining = sum([weights[i] for i in free]), spare
        for i in free:
            more = min(bound - given[i], max(1, remaining * weights[i] // whole), spare)
            given[i] = given[i] + more
            spare = spare - more
    return np.array([bound] + given)


def uneven_parts(own_key, count, total, reach, slope):
    if count == 2:
        one = jax.random.randint(own_key, (), max(1, total - reach), min(reach, total - 1) + 1)
        return jnp.stack([one, total - one])
    lengths = jnp.asarray(length_profile(count, total, reach, slope), jnp.int32)
    twos = (count - 1) // 2
    source_of, taker = lengths[1:1 + 2 * twos:2], lengths[2:2 + 2 * twos:2]
    slack = jnp.minimum(source_of - 1, reach - taker)
    moved = jax.random.randint(jax.random.fold_in(own_key, 1), (twos,), 0, 1 << 20) % (slack + 1)
    lengths = lengths.at[1:1 + 2 * twos:2].set(source_of - moved).at[2:2 + 2 * twos:2].set(taker + moved)
    return lengths[jax.random.permutation(jax.random.fold_in(own_key, 2), count)]


def scatter_about(key, extent, deviation, most, split=(), held_as=jnp.bfloat16):
    drawn = deviation * jax.random.normal(key, extent, jnp.float32)
    if split:
        drawn = drawn * level_of(key, extent, split, -0.22, 0.18)
    return jnp.clip(drawn, -most, most).astype(held_as)


def setup_inputs(seed: int = 0) -> dict:
    streams_of = jax.random.split(jax.random.key(seed), 12)
    prev_vector = scatter_about(streams_of[0], (NA, NB), 1.0, 6.0, ((0, 8), (1, 4)), jnp.float32)
    this_vector = scatter_about(streams_of[1], (NA, NB), 1.0, 6.0, ((0, 8), (1, 4)), jnp.float32)
    diagonal = jnp.clip(jax.random.uniform(streams_of[2], (NA, NB), jnp.float32, -0.5, 0.5) * level_of(streams_of[2], (NA, NB), ((0, 8), (1, 4)), -0.4, 0.0), -0.5, 0.5)
    alpha_blocks = scatter_about(streams_of[3], (NBLK_A, SLOTS, BLK, BLK), (3 * SLOTS * BLK) ** -0.5, 0.21875)
    alpha_classes = uneven_parts(streams_of[4], NCLS, NBLK_A, A_MOST, 1).astype(jnp.int32)
    alpha_offsets = place_ends(jax.random.randint(streams_of[5], (NBLK_A, SLOTS), 0, A_MOST), jax.random.fold_in(streams_of[5], 1), 0, A_MOST - 1).astype(jnp.int32)
    alpha_mask = place_ends((jax.random.randint(streams_of[6], (NBLK_A, SLOTS), 0, 4) < 3).astype(jnp.int32), jax.random.fold_in(streams_of[6], 1), 0, 1)
    beta_blocks = scatter_about(streams_of[7], (NBLK_B, SLOTS, BLK, BLK), (3 * SLOTS * BLK) ** -0.5, 0.21875)
    beta_classes = uneven_parts(streams_of[8], NCLS, NBLK_B, B_MOST, 1).astype(jnp.int32)
    beta_offsets = place_ends(jax.random.randint(streams_of[9], (NBLK_B, SLOTS), 0, B_MOST), jax.random.fold_in(streams_of[9], 1), 0, B_MOST - 1).astype(jnp.int32)
    beta_mask = place_ends((jax.random.randint(streams_of[10], (NBLK_B, SLOTS), 0, 4) < 3).astype(jnp.int32), jax.random.fold_in(streams_of[10], 1), 0, 1)
    return {"prev_vector": prev_vector, "this_vector": this_vector, "diagonal": diagonal, "alpha_blocks": alpha_blocks, "alpha_classes": alpha_classes, "alpha_offsets": alpha_offsets, "alpha_mask": alpha_mask, "beta_blocks": beta_blocks, "beta_classes": beta_classes, "beta_offsets": beta_offsets, "beta_mask": beta_mask}


def block_columns(class_sizes, offsets):
    class_ends = jnp.cumsum(class_sizes).astype(jnp.int32)
    class_starts = class_ends - class_sizes
    row_ids = jnp.arange(offsets.shape[0], dtype=jnp.int32)[:, None]
    inside = (row_ids >= class_starts[None, :]) & (row_ids < class_ends[None, :])
    first_block = jnp.sum(jnp.where(inside, class_starts[None, :], 0), axis=1).astype(jnp.int32)
    class_length = jnp.sum(jnp.where(inside, class_sizes[None, :], 0), axis=1).astype(jnp.int32)
    return (first_block[:, None] + offsets % class_length[:, None]).astype(jnp.int32)


def couple_first(values_in, blocks, columns, live_mask):
    block_count, slot_count, block_size, _ = blocks.shape
    width = values_in.shape[1]
    stacked = values_in.reshape(block_count, block_size, width)
    result = jnp.zeros((block_count, block_size, width), jnp.float32)
    for which_slot in range(slot_count):
        weights = blocks[:, which_slot].astype(jnp.float32) * live_mask[:, which_slot, None, None].astype(jnp.float32)
        picked = stacked[columns[:, which_slot]]
        result = result + jnp.einsum("rij,rjb->rib", weights, picked, precision=lax.Precision.HIGHEST)
    return result.reshape(block_count * block_size, width)


def reference(prev_vector, this_vector, diagonal, alpha_blocks, alpha_classes, alpha_offsets, alpha_mask, beta_blocks, beta_classes, beta_offsets, beta_mask):
    alpha_cols = block_columns(alpha_classes, alpha_offsets)
    beta_cols = block_columns(beta_classes, beta_offsets)
    previous = prev_vector
    current = this_vector
    produced = []
    for iteration in range(STEPS):
        rounded = current.astype(jnp.bfloat16).astype(jnp.float32)
        alpha_term = couple_first(rounded, alpha_blocks, alpha_cols, alpha_mask).astype(jnp.bfloat16)
        beta_term = couple_first(rounded.T, beta_blocks, beta_cols, beta_mask).T.astype(jnp.bfloat16)
        newer = 2.0 * (alpha_term.astype(jnp.float32) + beta_term.astype(jnp.float32) + diagonal * current) - previous
        previous = current
        current = newer
        produced.append(newer)
    return produced[0], produced[-1]
```

```python
import functools

import jax
import jax.numpy as jnp
from jax import lax
from jax.experimental import pallas as pl
from jax.experimental.pallas import tpu as pltpu
from jax.sharding import PartitionSpec as P

STEPS = 2
A_MOST = 8
B_MOST = 10
CHUNKS = 3
PAIR = 2

bf16 = jnp.bfloat16
f32 = jnp.float32
VM = pltpu.VMEM
SM = pltpu.SMEM


def block_columns(class_sizes, offsets):
    class_ends = jnp.cumsum(class_sizes)
    class_starts = class_ends - class_sizes
    row_ids = jnp.arange(offsets.shape[0], dtype=jnp.int32)[:, None]
    inside = (row_ids >= class_starts[None, :]) & (row_ids < class_ends[None, :])
    first_block = jnp.sum(jnp.where(inside, class_starts[None, :], 0), axis=1)
    class_length = jnp.sum(jnp.where(inside, class_sizes[None, :], 0), axis=1)
    return first_block[:, None] + offsets % class_length[:, None]


def most_crossing(most, slots):
    return max(min(most - rows, slots * rows) for rows in range(1, most))


def plan_indices(cols, live, group, per, halo):
    rows = jnp.arange(cols.shape[0], dtype=jnp.int32)
    groups = jnp.stack([group + 1, group - 1, group, group])
    bases = jnp.stack([group, group, group - 1, group + 1]) * per
    local = jnp.arange(per, dtype=jnp.int32)
    in_group = (rows[None, :] // per) == groups[:, None]
    hit = (
        (cols[None, :, :, None] == bases[:, None, None, None] + local)
        & in_group[:, :, None, None]
        & (live != 0)[None, :, :, None]
    )
    need = jnp.any(hit, axis=(1, 2)).astype(jnp.int32)
    rank = jnp.sum(jnp.where(local[None, :] < local[:, None], need[:, None, :], 0), axis=2)
    place = jnp.arange(halo, dtype=jnp.int32)
    send = jnp.sum(
        jnp.where((need[:2, None, :] != 0) & (rank[:2, None, :] == place[None, :, None]), local, 0),
        axis=2,
    )
    own_cols = lax.dynamic_slice_in_dim(cols, group * per, per, 0)
    own_live = lax.dynamic_slice_in_dim(live, group * per, per, 0)
    offset = own_cols - group * per

    def looked_up(ranks, shift):
        return jnp.sum(jnp.where(offset[:, :, None] + shift == local, ranks, 0), axis=2)

    place_of = jnp.where(
        offset < 0,
        looked_up(rank[2], per),
        jnp.where(offset < per, halo + offset, halo + per + looked_up(rank[3], -per)),
    )
    place_of = jnp.where(own_live != 0, place_of, 2 * halo + per)
    return send.astype(jnp.int32), place_of.astype(jnp.int32)


def pick_kernel(per, halo, blk, at_ref, send_ref, keep_ref, recv_ref, up_ref, down_ref, whole):
    own = keep_ref.shape[0]
    first = pl.multiple_of(at_ref[0] * own, 64)
    second = pl.multiple_of((1 - at_ref[0]) * own, 64)
    whole[pl.ds(first, own), :] = keep_ref[...]
    whole[pl.ds(second, own), :] = recv_ref[...]
    for place in range(halo):
        for way, out in enumerate((up_ref, down_ref)):
            start = pl.multiple_of(send_ref[way, place] * blk, blk)
            out[place * blk : (place + 1) * blk, :] = whole[pl.ds(start, blk), :]


def alpha_kernel(
    per, halo, blk, at_ref, table_ref, a_ref, keep_ref, recv_ref, low_ref, high_ref, own_ref, back_ref, ext, out
):
    own = keep_ref.shape[0]
    base = halo * blk
    at = at_ref[0]
    first = pl.multiple_of(at * own, 64)
    second = pl.multiple_of((1 - at) * own, 64)
    ext[0:base, :] = low_ref[...]
    ext[pl.ds(base + first, own), :] = keep_ref[...]
    ext[pl.ds(base + second, own), :] = recv_ref[...]
    top = base + per * blk
    ext[top : top + base, :] = high_ref[...]
    ext[top + base : top + base + blk, :] = jnp.zeros((blk, ext.shape[1]), ext.dtype)
    slots = a_ref.shape[1]
    for row in range(per):
        parts = [
            ext[pl.ds(pl.multiple_of(table_ref[row, slot] * blk, blk), blk), :] for slot in range(slots)
        ]
        weights = jnp.concatenate([a_ref[row, slot] for slot in range(slots)], axis=1)
        result = jnp.dot(weights, jnp.concatenate(parts, axis=0), preferred_element_type=f32)
        out[row * blk : (row + 1) * blk, :] = result.astype(bf16)
    own_ref[...] = out[pl.ds(first, own), :]
    back_ref[...] = out[pl.ds(second, own), :]


def beta_pick_kernel(halo, blk, send_ref, cur_ref, up_ref, down_ref):
    for place in range(halo):
        for way, out in enumerate((up_ref, down_ref)):
            start = pl.multiple_of(send_ref[way, place] * blk, blk)
            out[:, place * blk : (place + 1) * blk] = cur_ref[:, pl.ds(start, blk)].astype(bf16)


def beta_kernel(
    per, halo, blk, wide, at_ref, table_ref, b_ref, cur_ref, low_ref, high_ref, diag_ref, prev_ref, out_ref, ext
):
    step = pl.program_id(0)
    base = halo * blk
    top = base + per * blk

    @pl.when(step == 0)
    def _():
        ext[:, 0:base] = low_ref[...]
        for j in range(per):
            ext[:, base + j * blk : base + (j + 1) * blk] = cur_ref[:, j * blk : (j + 1) * blk].astype(bf16)
        ext[:, top : top + base] = high_ref[...]
        ext[:, top + base : top + base + blk] = jnp.zeros((ext.shape[0], blk), ext.dtype)

    slots = b_ref.shape[1]
    for one in range(wide):
        row = step * wide + one
        parts = [
            ext[:, pl.ds(pl.multiple_of(table_ref[row, slot] * blk, blk), blk)] for slot in range(slots)
        ]
        weights = jnp.concatenate([b_ref[one, slot] for slot in range(slots)], axis=1)
        term = lax.dot_general(
            jnp.concatenate(parts, axis=1), weights, (((1,), (1,)), ((), ())), preferred_element_type=f32
        ).astype(bf16).astype(f32)
        here = slice(one * blk, (one + 1) * blk)
        cur = cur_ref[:, pl.ds(pl.multiple_of(row * blk, blk), blk)]
        out_ref[:, here] = 2.0 * (term + diag_ref[:, here] * cur) - prev_ref[:, here]


def combine_kernel(rounds, at_ref, rest_ref, own_ref, recv_ref, *refs):
    out_ref = refs[-3] if rounds else refs[-1]
    for way, alpha_ref in enumerate((own_ref, recv_ref)):

        @pl.when(pl.program_id(0) == way)
        def _():
            newer = rest_ref[...] + 2.0 * alpha_ref[...].astype(f32)
            out_ref[...] = newer
            if rounds:
                refs[way - 2][...] = newer.astype(bf16)


def cost(flops, moved):
    return pl.CostEstimate(flops=flops, bytes_accessed=moved, transcendentals=0)


def halo_on_device(
    prev_vector,
    this_vector,
    diagonal,
    alpha_blocks,
    alpha_classes,
    alpha_offsets,
    alpha_mask,
    beta_blocks,
    beta_classes,
    beta_offsets,
    beta_mask,
):
    alpha_count = lax.axis_size("aa")
    beta_count = lax.axis_size("ba")
    own_alpha, own_beta = prev_vector.shape
    blk = alpha_blocks.shape[-1]
    slots = alpha_blocks.shape[1]
    a_per = PAIR * own_alpha // blk
    b_per = own_beta // blk
    a_halo = most_crossing(A_MOST, slots)
    b_halo = most_crossing(B_MOST, slots)
    half = own_beta // PAIR
    w = half // CHUNKS

    at_aa = lax.axis_index("aa")
    at_ba = lax.axis_index("ba")
    side = at_aa % PAIR
    pair = at_aa // PAIR
    swap = [(i, i ^ 1) for i in range(alpha_count)]
    a_up = [(i, i + PAIR) for i in range(alpha_count - PAIR)]
    a_down = [(i + PAIR, i) for i in range(alpha_count - PAIR)]
    b_up = [(i, i + 1) for i in range(beta_count - 1)]
    b_down = [(i + 1, i) for i in range(beta_count - 1)]

    def first_pieces(chunk):
        def piece(which):
            return lax.dynamic_slice(this_vector, (0, which * half + chunk * w), (own_alpha, w)).astype(bf16)

        return piece(side), piece(1 - side)

    a_send, a_table = plan_indices(block_columns(alpha_classes, alpha_offsets), alpha_mask, pair, a_per, a_halo)
    b_send, b_table = plan_indices(block_columns(beta_classes, beta_offsets), beta_mask, at_ba, b_per, b_halo)
    side_at = jnp.reshape(side, (1,)).astype(jnp.int32)
    own_a = lax.dynamic_slice_in_dim(alpha_blocks, pair * a_per, a_per, 0)
    ba_at = jnp.reshape(at_ba, (1,)).astype(jnp.int32)

    smem = pl.BlockSpec(memory_space=SM)
    vmem = pl.BlockSpec(memory_space=VM)

    def shape(rows, columns, dtype=bf16):
        return jax.ShapeDtypeStruct((rows, columns), dtype)

    pick = pl.pallas_call(
        functools.partial(pick_kernel, a_per, a_halo, blk),
        out_shape=[shape(a_halo * blk, w)] * 2,
        in_specs=[smem, smem, vmem, vmem],
        out_specs=[vmem, vmem],
        scratch_shapes=[VM((a_per * blk, w), bf16)],
        cost_estimate=cost(0, 4 * a_halo * blk * w),
        name="pick",
    )
    alpha = pl.pallas_call(
        functools.partial(alpha_kernel, a_per, a_halo, blk),
        out_shape=[shape(own_alpha, w)] * 2,
        in_specs=[smem, smem] + [vmem] * 5,
        out_specs=[vmem, vmem],
        scratch_shapes=[VM(((2 * a_halo + a_per + 1) * blk, w), bf16), VM((a_per * blk, w), bf16)],
        cost_estimate=cost(2 * a_per * slots * blk * blk * w, 8 * own_alpha * w),
        name="alpha",
    )
    beta_pick = pl.pallas_call(
        functools.partial(beta_pick_kernel, b_halo, blk),
        out_shape=[shape(own_alpha, b_halo * blk)] * 2,
        in_specs=[smem, vmem],
        out_specs=[vmem, vmem],
        cost_estimate=cost(0, 4 * own_alpha * own_beta),
        name="beta_pick",
    )
    wide = 2
    whole = lambda r, at, table: (0, 0)
    tile = lambda r, at, table: (0, r)
    beta = pl.pallas_call(
        functools.partial(beta_kernel, b_per, b_halo, blk, wide),
        out_shape=shape(own_alpha, own_beta, f32),
        grid_spec=pltpu.PrefetchScalarGridSpec(
            num_scalar_prefetch=2,
            grid=(b_per // wide,),
            in_specs=[
                pl.BlockSpec((wide, slots, blk, blk), lambda r, at, table: (at[0] * (b_per // wide) + r, 0, 0, 0)),
                pl.BlockSpec((own_alpha, own_beta), whole, pipeline_mode=pl.Buffered(1)),
                pl.BlockSpec((own_alpha, b_halo * blk), whole, pipeline_mode=pl.Buffered(1)),
                pl.BlockSpec((own_alpha, b_halo * blk), whole, pipeline_mode=pl.Buffered(1)),
                pl.BlockSpec((own_alpha, wide * blk), tile),
                pl.BlockSpec((own_alpha, wide * blk), tile),
            ],
            out_specs=pl.BlockSpec((own_alpha, wide * blk), tile),
            scratch_shapes=[VM((own_alpha, (2 * b_halo + b_per + 1) * blk), bf16)],
        ),
        cost_estimate=cost(2 * b_per * slots * blk * blk * own_alpha, 16 * own_alpha * own_beta),
        name="beta",
    )

    def combine(chunk, rounds, rest, own_term, recv_term, so_far):
        def spot(g, at):
            return (0, jnp.where(g == 0, at[0], 1 - at[0]) * CHUNKS + chunk)

        full = pl.BlockSpec((own_alpha, w), lambda g, at: (0, 0))
        piece = pl.BlockSpec((own_alpha, w), spot)
        operands = [side_at, rest, own_term, recv_term]
        in_specs = [piece, full, full]
        aliases = {}
        if so_far is not None:
            aliases = {len(operands): 0}
            operands.append(so_far)
            in_specs.append(pl.BlockSpec(memory_space=pl.ANY))
        out_shape = [shape(own_alpha, own_beta, f32)]
        out_specs = [piece]
        if rounds:
            out_shape += [shape(own_alpha, w)] * 2
            out_specs += [full] * 2
        return pl.pallas_call(
            functools.partial(combine_kernel, rounds),
            out_shape=out_shape,
            grid_spec=pltpu.PrefetchScalarGridSpec(
                num_scalar_prefetch=1, grid=(PAIR,), in_specs=in_specs, out_specs=out_specs
            ),
            input_output_aliases=aliases,
            cost_estimate=cost(4 * own_alpha * w, 24 * own_alpha * w),
            name="combine",
        )(*operands)

    previous, current = prev_vector, this_vector
    pieces = [first_pieces(chunk) for chunk in range(CHUNKS)]
    produced = []
    for iteration in range(STEPS):
        received = [lax.ppermute(send, "aa", swap) for _, send in pieces]
        up, down = beta_pick(b_send, current)
        low = lax.ppermute(up, "ba", b_up)
        high = lax.ppermute(down, "ba", b_down)
        halos = []
        for chunk in range(CHUNKS):
            up, down = pick(side_at, a_send, pieces[chunk][0], received[chunk])
            halos.append((lax.ppermute(up, "aa", a_up), lax.ppermute(down, "aa", a_down)))
        rest = beta(ba_at, b_table, beta_blocks, current, low, high, diagonal, previous)
        terms = []
        for chunk in range(CHUNKS):
            own_term, back = alpha(side_at, a_table, own_a, pieces[chunk][0], received[chunk], *halos[chunk])
            terms.append((own_term, lax.ppermute(back, "aa", swap)))
        newer = None
        rounds = iteration < STEPS - 1
        fresh = []
        for chunk in range(CHUNKS):
            newer, *pair_pieces = combine(chunk, rounds, rest, *terms[chunk], newer)
            fresh.append(tuple(pair_pieces))
        pieces = fresh
        previous, current = current, newer
        produced.append(newer)
    return (produced[0], produced[-1])


def couple_last(pieces, blocks, columns, live_mask):
    out_blocks, slot_count, block_size, _ = blocks.shape
    item_count = pieces.shape[0]
    stacked = pieces.reshape(item_count, -1, block_size)
    picked = stacked[:, columns, :] * live_mask[None, :, :, None]
    result = jnp.einsum("crkj,rkij->cri", picked, blocks, preferred_element_type=jnp.float32)
    return result.reshape(item_count, out_blocks * block_size).astype(jnp.bfloat16)


def whole_on_device(
    prev_vector,
    this_vector,
    diagonal,
    alpha_blocks,
    alpha_classes,
    alpha_offsets,
    alpha_mask,
    beta_blocks,
    beta_classes,
    beta_offsets,
    beta_mask,
):
    alpha_cols = block_columns(alpha_classes, alpha_offsets)
    alpha_live = alpha_mask.astype(jnp.bfloat16)
    beta_cols = block_columns(beta_classes, beta_offsets)
    beta_live = beta_mask.astype(jnp.bfloat16)
    alpha_count = lax.axis_size("aa")
    beta_count = lax.axis_size("ba")
    own_alpha, own_beta = prev_vector.shape
    own_count = beta_blocks.shape[0] // beta_count
    first_own = lax.axis_index("ba") * own_count
    own_blocks = lax.dynamic_slice_in_dim(beta_blocks, first_own, own_count, 0)
    own_cols = lax.dynamic_slice_in_dim(beta_cols, first_own, own_count, 0)
    own_live = lax.dynamic_slice_in_dim(beta_live, first_own, own_count, 0)
    previous = prev_vector
    current = this_vector
    produced = []
    for iteration in range(STEPS):
        rounded = current.astype(jnp.bfloat16)
        alpha_shaped = rounded.reshape(own_alpha, alpha_count, own_beta // alpha_count)
        pieces = lax.all_to_all(alpha_shaped, "aa", split_axis=1, concat_axis=0, tiled=True)
        whole_alpha, single, columns_here = pieces.shape
        flat = pieces.reshape(whole_alpha, columns_here)
        applied = couple_last(flat.T, alpha_blocks, alpha_cols, alpha_live).T
        alpha_local = applied.reshape(whole_alpha, single, columns_here)
        alpha_back = lax.all_to_all(alpha_local, "aa", split_axis=0, concat_axis=1, tiled=True)
        alpha_term = alpha_back.reshape(own_alpha, own_beta)
        whole_rows = lax.all_gather(rounded, "ba", axis=1, tiled=True)
        beta_term = couple_last(whole_rows, own_blocks, own_cols, own_live)
        newer = (
            2.0
            * (alpha_term.astype(jnp.float32) + beta_term.astype(jnp.float32) + diagonal * current)
            - previous
        )
        previous = current
        current = newer
        produced.append(newer)
    return (produced[0], produced[-1])


def on_device(*args):
    own_alpha, own_beta = args[0].shape
    blk = args[3].shape[-1]
    fits = (
        lax.axis_size("aa") % PAIR == 0
        and (PAIR * own_alpha) % blk == 0
        and PAIR * own_alpha // blk >= A_MOST - 1
        and own_beta % (PAIR * CHUNKS * blk) == 0
        and own_beta // blk >= B_MOST - 1
    )
    return (halo_on_device if fits else whole_on_device)(*args)


def solution(mesh):
    return jax.shard_map(
        on_device,
        mesh=mesh,
        in_specs=(P("aa", "ba"),) * 3 + (P(),) * 8,
        out_specs=(P("aa", "ba"), P("aa", "ba")),
        check_vma=False,
    )
```

```python
import functools

import jax
import jax.numpy as jnp
from jax import lax
from jax.experimental import pallas as pl
from jax.experimental.pallas import tpu as pltpu
from jax.sharding import PartitionSpec as P

STEPS = 2
A_MOST = 8
B_MOST = 10
CHUNKS = 2
PAIR = 2

bf16 = jnp.bfloat16
f32 = jnp.float32
i32 = jnp.int32
VM = pltpu.VMEM
SM = pltpu.SMEM
MIB = 1 << 20


def most_needed(most, slots, rows, blocks):
    best = 0
    for length in range(1, most + 1):
        for start in range(min(rows[0], blocks[0]) - most, max(sum(rows), sum(blocks))):
            held = [
                max(0, min(start + length, sum(part)) - max(start, part[0])) for part in (rows, blocks)
            ]
            best = max(best, min(slots * held[0], held[1]))
    return best


class Spots:
    def __init__(self, slots, a_rows, a_big, a_small, b_per, b_halo):
        self.size = 0
        self.side = self.take(1)
        self.big = self.take(a_big)
        self.small = self.take(a_small)
        self.a_table = self.take(a_rows * slots)
        self.b_up = self.take(b_halo)
        self.b_down = self.take(b_halo)
        self.b_table = self.take(b_per * slots)

    def take(self, count):
        first = self.size
        self.size += count
        return first


def index_kernel(plan, at_ref, ac_ref, ao_ref, am_ref, bc_ref, bo_ref, bm_ref, out_ref, a_cols, b_cols, rank):
    spots, slots, a_per, a_rows, a_big, a_small, b_per, b_halo = plan
    side, pair, at_ba = at_ref[0], at_ref[1], at_ref[2]
    out_ref[spots.side] = side

    def columns(classes_ref, offsets_ref, cols):
        def one_class(c, start):
            length = classes_ref[c]

            def one_row(r, _):
                for slot in range(slots):
                    cols[slot, start + r] = start + lax.rem(offsets_ref[slot, start + r], length)
                return 0

            lax.fori_loop(0, length, one_row, 0)
            return start + length

        lax.fori_loop(0, classes_ref.shape[0], one_class, 0)

    columns(ac_ref, ao_ref, a_cols)
    columns(bc_ref, bo_ref, b_cols)

    def ranked(cols, mask_ref, first_row, row_count, base, per, where, room, keep):
        for j in range(per):
            rank[keep, j] = 0
        total = cols.shape[1]

        def mark(r, _):
            row = jnp.clip(first_row + r, 0, total - 1)
            fits = (first_row + r >= 0) & (first_row + r < total)
            for slot in range(slots):
                local = cols[slot, row] - base

                @pl.when(fits & (mask_ref[slot, row] != 0) & (local >= 0) & (local < per))
                def _():
                    rank[keep, jnp.clip(local, 0, per - 1)] = 1

            return 0

        lax.fori_loop(0, row_count, mark, 0)
        if where is not None:
            for place in range(room):
                out_ref[where + place] = 0

        count = 0
        for j in range(per):
            used = rank[keep, j]
            if where is not None:

                @pl.when(used != 0)
                def _():
                    out_ref[where + jnp.minimum(count, room - 1)] = j

            rank[keep, j] = count
            count = count + used

    def tabled(cols, mask_ref, first_row, row_count, base, per, low_first, own_first, high_first, zero, where):
        def one_row(r, _):
            for slot in range(slots):
                local = cols[slot, first_row + r] - base
                low = low_first + rank[0, jnp.clip(local + per, 0, per - 1)]
                high = high_first + rank[1, jnp.clip(local - per, 0, per - 1)]
                place = jnp.where(local < 0, low, jnp.where(local < per, own_first + local, high))
                live = mask_ref[slot, first_row + r] != 0
                out_ref[where + r * slots + slot] = jnp.where(live, place, zero)
            return 0

        lax.fori_loop(0, row_count, one_row, 0)

    away = 1 - 2 * side
    skip = (a_per - a_rows) * side
    a_first = pair * a_per + skip
    base = pair * a_per
    ranked(a_cols, am_ref, a_first + away * a_per, a_rows, base, a_per, spots.big, a_big, 2)
    ranked(a_cols, am_ref, a_first - away * a_per, a_rows, base, a_per, spots.small, a_small, 2)
    ranked(a_cols, am_ref, a_first, a_rows, base - a_per, a_per, None, 0, 0)
    ranked(a_cols, am_ref, a_first, a_rows, base + a_per, a_per, None, 0, 1)
    top = a_big + a_per
    tabled(
        a_cols,
        am_ref,
        a_first,
        a_rows,
        base,
        a_per,
        jnp.where(side == 0, 0, top),
        a_big,
        jnp.where(side == 0, top, 0),
        top + a_small,
        spots.a_table,
    )
    base = at_ba * b_per
    ranked(b_cols, bm_ref, base + b_per, b_per, base, b_per, spots.b_up, b_halo, 2)
    ranked(b_cols, bm_ref, base - b_per, b_per, base, b_per, spots.b_down, b_halo, 2)
    ranked(b_cols, bm_ref, base, b_per, base - b_per, b_per, None, 0, 0)
    ranked(b_cols, bm_ref, base, b_per, base + b_per, b_per, None, 0, 1)
    tabled(
        b_cols, bm_ref, base, b_per, base, b_per, 0, b_halo, b_halo + b_per, 2 * b_halo + b_per, spots.b_table
    )


def spot_of(ref, place, blk):
    return pl.ds(pl.multiple_of(ref[place] * blk, blk), blk)


def merge(side, first, keep_ref, recv_ref, into):
    own = keep_ref.shape[0]
    step = 64 if own % 64 == 0 else 16
    into[pl.ds(pl.multiple_of(first + side * own, step), own), :] = keep_ref[...]
    into[pl.ds(pl.multiple_of(first + (1 - side) * own, step), own), :] = recv_ref[...]


def pick_kernel(spots, a_big, a_small, blk, index_ref, keep_ref, recv_ref, big_ref, small_ref, whole):
    merge(index_ref[spots.side], 0, keep_ref, recv_ref, whole)
    for count, first, out in ((a_big, spots.big, big_ref), (a_small, spots.small, small_ref)):
        for place in range(count):
            out[place * blk : (place + 1) * blk, :] = whole[spot_of(index_ref, first + place, blk), :]


def alpha_kernel(
    spots, plan, rounds, index_ref, a_ref, keep_ref, recv_ref, big_ref, small_ref, rest_ref, *refs
):
    a_per, a_rows, a_big, a_small, blk = plan
    ext, term = refs[-2:]
    outs = refs[-4:-2] if rounds else refs[-3:-2]
    side = index_ref[spots.side]
    own = keep_ref.shape[0]
    top = (a_big + a_per) * blk
    end = top + a_small * blk
    ext[0 : a_big * blk, :] = big_ref[...]
    merge(side, a_big * blk, keep_ref, recv_ref, ext)
    ext[top:end, :] = small_ref[...]
    ext[end : end + blk, :] = jnp.zeros((blk, ext.shape[1]), ext.dtype)
    slots = a_ref.shape[1]
    for row in range(a_rows):
        parts = [ext[spot_of(index_ref, spots.a_table + row * slots + slot, blk), :] for slot in range(slots)]
        weights = jnp.concatenate([a_ref[row, slot] for slot in range(slots)], axis=1)
        result = jnp.dot(weights, jnp.concatenate(parts, axis=0), preferred_element_type=f32)
        term[row * blk : (row + 1) * blk, :] = result.astype(bf16)
    shift = a_rows * blk - own
    alpha = term[pl.ds(pl.multiple_of(side * shift, 16), own), :].astype(f32)
    newer = rest_ref[...] + 2.0 * alpha
    outs[0][...] = newer
    if rounds:
        outs[1][...] = newer.astype(bf16)


def beta_pick_kernel(spots, b_halo, blk, index_ref, *refs):
    up_ref, down_ref, whole = refs[-3:]
    at = 0
    for chunk in refs[:-3]:
        whole[:, at : at + chunk.shape[1]] = chunk[...]
        at += chunk.shape[1]
    for first, out in ((spots.b_up, up_ref), (spots.b_down, down_ref)):
        for place in range(b_halo):
            out[:, place * blk : (place + 1) * blk] = whole[:, spot_of(index_ref, first + place, blk)]


def beta_kernel(spots, plan, index_ref, at_ref, b_ref, *refs):
    b_per, b_halo, blk, wide = plan
    low_ref, high_ref, cur_ref, diag_ref, prev_ref, out_ref, ext = refs[-7:]
    step = pl.program_id(0)
    base = b_halo * blk
    top = base + b_per * blk

    @pl.when(step == 0)
    def _():
        ext[:, 0:base] = low_ref[...]
        at = base
        for chunk in refs[:-7]:
            ext[:, at : at + chunk.shape[1]] = chunk[...]
            at += chunk.shape[1]
        ext[:, top : top + base] = high_ref[...]
        ext[:, top + base : top + base + blk] = jnp.zeros((ext.shape[0], blk), ext.dtype)

    slots = b_ref.shape[1]
    for one in range(wide):
        first = spots.b_table + (step * wide + one) * slots
        parts = [ext[:, spot_of(index_ref, first + slot, blk)] for slot in range(slots)]
        weights = jnp.concatenate([b_ref[one, slot] for slot in range(slots)], axis=1)
        term = lax.dot_general(
            jnp.concatenate(parts, axis=1), weights, (((1,), (1,)), ((), ())), preferred_element_type=f32
        ).astype(bf16).astype(f32)
        here = slice(one * blk, (one + 1) * blk)
        out_ref[:, here] = 2.0 * (term + diag_ref[:, here] * cur_ref[:, here]) - prev_ref[:, here]


def cost(flops, moved):
    return pl.CostEstimate(flops=flops, bytes_accessed=moved, transcendentals=0)


def limit(mib):
    return pltpu.CompilerParams(vmem_limit_bytes=mib * MIB)


def halo_on_device(
    prev_vector,
    this_vector,
    diagonal,
    alpha_blocks,
    alpha_classes,
    alpha_offsets,
    alpha_mask,
    beta_blocks,
    beta_classes,
    beta_offsets,
    beta_mask,
):
    alpha_count = lax.axis_size("aa")
    beta_count = lax.axis_size("ba")
    own_alpha, own_beta = prev_vector.shape
    row_blocks, slots, blk, _ = alpha_blocks.shape
    a_per = PAIR * own_alpha // blk
    a_rows = -(-own_alpha // blk)
    b_per = own_beta // blk
    need = functools.partial(most_needed, A_MOST, slots)
    a_big = need((0, a_rows), (-a_per, a_per))
    a_small = need((0, a_rows), (a_per, a_per))
    b_halo = most_needed(B_MOST, slots, (0, b_per), (b_per, b_per))
    spots = Spots(slots, a_rows, a_big, a_small, b_per, b_halo)
    w = own_beta // CHUNKS
    tile = min(w, 256)
    tiles = w // tile

    at_aa = lax.axis_index("aa")
    at_ba = lax.axis_index("ba")
    side = at_aa % PAIR
    pair = at_aa // PAIR
    swap = [(i, i ^ 1) for i in range(alpha_count)]
    far = range(alpha_count - PAIR)
    big_way = [(i, i + PAIR) if i % PAIR == 0 else (i + PAIR, i) for i in far]
    small_way = [(i + PAIR, i) if i % PAIR == 0 else (i, i + PAIR) for i in far]
    b_up = [(i, i + 1) for i in range(beta_count - 1)]
    b_down = [(i + 1, i) for i in range(beta_count - 1)]

    smem = pl.BlockSpec(memory_space=SM)
    vmem = pl.BlockSpec(memory_space=VM)

    def shape(rows, columns, dtype=bf16):
        return jax.ShapeDtypeStruct((rows, columns), dtype)

    index = pl.pallas_call(
        functools.partial(index_kernel, (spots, slots, a_per, a_rows, a_big, a_small, b_per, b_halo)),
        out_shape=jax.ShapeDtypeStruct((spots.size,), i32),
        in_specs=[smem] * 7,
        out_specs=smem,
        scratch_shapes=[
            SM((slots, row_blocks), i32),
            SM((slots, beta_blocks.shape[0]), i32),
            SM((3, max(a_per, b_per)), i32),
        ],
        compiler_params=limit(4),
        cost_estimate=cost(10_000_000, 1_000_000),
        name="index",
    )(
        jnp.stack([side, pair, at_ba]).astype(i32),
        alpha_classes,
        alpha_offsets.T,
        alpha_mask.T,
        beta_classes,
        beta_offsets.T,
        beta_mask.T,
    )
    own_a = lax.dynamic_slice_in_dim(alpha_blocks, pair * a_per + side * (a_per - a_rows), a_rows, 0)
    ba_at = jnp.reshape(at_ba, (1,)).astype(i32)

    def column(rows, which=0):
        return pl.BlockSpec((rows, tile), lambda g, *_: (0, which + g))

    pick = pl.pallas_call(
        functools.partial(pick_kernel, spots, a_big, a_small, blk),
        out_shape=[shape(a_big * blk, w), shape(a_small * blk, w)],
        grid_spec=pltpu.PrefetchScalarGridSpec(
            num_scalar_prefetch=1,
            grid=(tiles,),
            in_specs=[column(own_alpha)] * 2,
            out_specs=[column(a_big * blk), column(a_small * blk)],
            scratch_shapes=[VM((a_per * blk, tile), bf16)],
        ),
        compiler_params=limit(8),
        cost_estimate=cost(0, 2 * (PAIR * own_alpha + (a_big + a_small) * blk) * w),
        name="pick",
    )
    beta_pick = pl.pallas_call(
        functools.partial(beta_pick_kernel, spots, b_halo, blk),
        out_shape=[shape(own_alpha, b_halo * blk)] * 2,
        in_specs=[smem] + [vmem] * CHUNKS,
        out_specs=[vmem, vmem],
        scratch_shapes=[VM((own_alpha, own_beta), bf16)],
        compiler_params=limit(12),
        cost_estimate=cost(0, 4 * own_alpha * own_beta),
        name="beta_pick",
    )
    wide = 2
    whole = lambda r, index, at: (0, 0)
    strip = pl.BlockSpec((own_alpha, wide * blk), lambda r, index, at: (0, r))
    once = pl.Buffered(1)
    beta = pl.pallas_call(
        functools.partial(beta_kernel, spots, (b_per, b_halo, blk, wide)),
        out_shape=shape(own_alpha, own_beta, f32),
        grid_spec=pltpu.PrefetchScalarGridSpec(
            num_scalar_prefetch=2,
            grid=(b_per // wide,),
            in_specs=[
                pl.BlockSpec(
                    (wide, slots, blk, blk), lambda r, index, at: (at[0] * (b_per // wide) + r, 0, 0, 0)
                )
            ]
            + [pl.BlockSpec((own_alpha, w), whole, pipeline_mode=once)] * CHUNKS
            + [pl.BlockSpec((own_alpha, b_halo * blk), whole, pipeline_mode=once)] * 2
            + [strip] * 3,
            out_specs=strip,
            scratch_shapes=[VM((own_alpha, (2 * b_halo + b_per + 1) * blk), bf16)],
        ),
        compiler_params=limit(20),
        cost_estimate=cost(2 * b_per * slots * blk * blk * own_alpha, 16 * own_alpha * own_beta),
        name="beta",
    )

    def alpha(chunk, rounds, keep, recv, big, small, rest, so_far):
        operands = [index, own_a, keep, recv, big, small, rest]
        in_specs = [
            pl.BlockSpec((a_rows, slots, blk, blk), lambda g, _: (0, 0, 0, 0)),
            column(own_alpha),
            column(own_alpha),
            column(a_big * blk),
            column(a_small * blk),
            column(own_alpha, chunk * tiles),
        ]
        aliases = {}
        if so_far is not None:
            aliases = {len(operands): 0}
            operands.append(so_far)
            in_specs.append(pl.BlockSpec(memory_space=pl.ANY))
        out_shape = [shape(own_alpha, own_beta, f32)]
        out_specs = [column(own_alpha, chunk * tiles)]
        if rounds:
            out_shape.append(shape(own_alpha, w))
            out_specs.append(column(own_alpha))
        return pl.pallas_call(
            functools.partial(alpha_kernel, spots, (a_per, a_rows, a_big, a_small, blk), rounds),
            out_shape=out_shape,
            grid_spec=pltpu.PrefetchScalarGridSpec(
                num_scalar_prefetch=1,
                grid=(tiles,),
                in_specs=in_specs,
                out_specs=out_specs,
                scratch_shapes=[
                    VM(((a_big + a_per + a_small + 1) * blk, tile), bf16),
                    VM((a_rows * blk, tile), bf16),
                ],
            ),
            input_output_aliases=aliases,
            compiler_params=limit(14),
            cost_estimate=cost(2 * a_rows * slots * blk * blk * w, 16 * own_alpha * w),
            name="alpha",
        )(*operands)

    previous, current = prev_vector, this_vector
    pieces = [this_vector[:, chunk * w : (chunk + 1) * w].astype(bf16) for chunk in range(CHUNKS)]
    produced = []
    for iteration in range(STEPS):
        received = [lax.ppermute(piece, "aa", swap) for piece in pieces]
        up, down = beta_pick(index, *pieces)
        low = lax.ppermute(up, "ba", b_up)
        high = lax.ppermute(down, "ba", b_down)
        halos = []
        for chunk in range(CHUNKS):
            big, small = pick(index, pieces[chunk], received[chunk])
            halos.append((lax.ppermute(big, "aa", big_way), lax.ppermute(small, "aa", small_way)))
        rest = beta(index, ba_at, beta_blocks, *pieces, low, high, current, diagonal, previous)
        newer = None
        rounds = iteration < STEPS - 1
        fresh = []
        for chunk in range(CHUNKS):
            newer, *piece = alpha(chunk, rounds, pieces[chunk], received[chunk], *halos[chunk], rest, newer)
            fresh += piece
        pieces = fresh
        previous, current = current, newer
        produced.append(newer)
    return (produced[0], produced[-1])


def block_columns(class_sizes, offsets):
    class_ends = jnp.cumsum(class_sizes)
    class_starts = class_ends - class_sizes
    row_ids = jnp.arange(offsets.shape[0], dtype=jnp.int32)[:, None]
    inside = (row_ids >= class_starts[None, :]) & (row_ids < class_ends[None, :])
    first_block = jnp.sum(jnp.where(inside, class_starts[None, :], 0), axis=1)
    class_length = jnp.sum(jnp.where(inside, class_sizes[None, :], 0), axis=1)
    return first_block[:, None] + offsets % class_length[:, None]


def couple_last(pieces, blocks, columns, live_mask):
    out_blocks, slot_count, block_size, _ = blocks.shape
    item_count = pieces.shape[0]
    stacked = pieces.reshape(item_count, -1, block_size)
    picked = stacked[:, columns, :] * live_mask[None, :, :, None]
    result = jnp.einsum("crkj,rkij->cri", picked, blocks, preferred_element_type=jnp.float32)
    return result.reshape(item_count, out_blocks * block_size).astype(jnp.bfloat16)


def whole_on_device(
    prev_vector,
    this_vector,
    diagonal,
    alpha_blocks,
    alpha_classes,
    alpha_offsets,
    alpha_mask,
    beta_blocks,
    beta_classes,
    beta_offsets,
    beta_mask,
):
    alpha_cols = block_columns(alpha_classes, alpha_offsets)
    alpha_live = alpha_mask.astype(jnp.bfloat16)
    beta_cols = block_columns(beta_classes, beta_offsets)
    beta_live = beta_mask.astype(jnp.bfloat16)
    alpha_count = lax.axis_size("aa")
    beta_count = lax.axis_size("ba")
    own_alpha, own_beta = prev_vector.shape
    own_count = beta_blocks.shape[0] // beta_count
    first_own = lax.axis_index("ba") * own_count
    own_blocks = lax.dynamic_slice_in_dim(beta_blocks, first_own, own_count, 0)
    own_cols = lax.dynamic_slice_in_dim(beta_cols, first_own, own_count, 0)
    own_live = lax.dynamic_slice_in_dim(beta_live, first_own, own_count, 0)
    previous = prev_vector
    current = this_vector
    produced = []
    for iteration in range(STEPS):
        rounded = current.astype(jnp.bfloat16)
        alpha_shaped = rounded.reshape(own_alpha, alpha_count, own_beta // alpha_count)
        pieces = lax.all_to_all(alpha_shaped, "aa", split_axis=1, concat_axis=0, tiled=True)
        whole_alpha, single, columns_here = pieces.shape
        flat = pieces.reshape(whole_alpha, columns_here)
        applied = couple_last(flat.T, alpha_blocks, alpha_cols, alpha_live).T
        alpha_local = applied.reshape(whole_alpha, single, columns_here)
        alpha_back = lax.all_to_all(alpha_local, "aa", split_axis=0, concat_axis=1, tiled=True)
        alpha_term = alpha_back.reshape(own_alpha, own_beta)
        whole_rows = lax.all_gather(rounded, "ba", axis=1, tiled=True)
        beta_term = couple_last(whole_rows, own_blocks, own_cols, own_live)
        newer = (
            2.0
            * (alpha_term.astype(jnp.float32) + beta_term.astype(jnp.float32) + diagonal * current)
            - previous
        )
        previous = current
        current = newer
        produced.append(newer)
    return (produced[0], produced[-1])


def on_device(*args):
    own_alpha, own_beta = args[0].shape
    blk = args[3].shape[-1]
    fits = (
        lax.axis_size("aa") % PAIR == 0
        and (PAIR * own_alpha) % blk == 0
        and PAIR * own_alpha // blk >= A_MOST - 1
        and own_beta % (2 * CHUNKS * blk) == 0
        and own_beta // blk >= B_MOST - 1
    )
    return (halo_on_device if fits else whole_on_device)(*args)


def solution(mesh):
    return jax.shard_map(
        on_device,
        mesh=mesh,
        in_specs=(P("aa", "ba"),) * 3 + (P(),) * 8,
        out_specs=(P("aa", "ba"), P("aa", "ba")),
        check_vma=False,
    )
```

```python
import functools

import jax
import jax.numpy as jnp
from jax import lax
from jax.experimental import pallas as pl
from jax.experimental.pallas import tpu as pltpu
from jax.sharding import PartitionSpec as P


STEPS = 2
A_MOST = 8
B_MOST = 10
A_MAIN = 3
SHARES = (1, 1)
ORDER = (("p0", "b", "a0", "p1", "a1"), ("p0", "b", "p1", "a0", "a1"))
PAIR = 2

bf16 = jnp.bfloat16
f32 = jnp.float32
i32 = jnp.int32
VM = pltpu.VMEM
SM = pltpu.SMEM
MIB = 1 << 20


def most_needed(most, slots, rows, blocks):
    best = 0
    for length in range(1, most + 1):
        for start in range(min(rows[0], blocks[0]) - most, max(sum(rows), sum(blocks))):
            held = [
                max(0, min(start + length, sum(part)) - max(start, part[0])) for part in (rows, blocks)
            ]
            best = max(best, min(slots * held[0], held[1]))
    return best


class Spots:
    def __init__(self, slots, a_rows, a_halo, b_per, b_halo):
        self.size = 0
        self.side = self.take(1)
        self.a_lists = [self.take(a_halo), self.take(a_halo)]
        self.a_table = self.take(a_rows * slots)
        self.b_lists = [self.take(b_halo), self.take(b_halo)]
        self.b_table = self.take(b_per * slots)

    def take(self, count):
        first = self.size
        self.size += count
        return first


def partners(group):
    odd = lax.rem(group, 2)
    return group + 1 - 2 * odd, group - 1 + 2 * odd


def columns(slots, classes_ref, offsets_ref, cols):
    def one_class(c, start):
        length = classes_ref[c]

        def one_row(r, _):
            for slot in range(slots):
                cols[slot, start + r] = start + lax.rem(offsets_ref[slot, start + r], length)
            return 0

        lax.fori_loop(0, length, one_row, 0)
        return start + length

    lax.fori_loop(0, classes_ref.shape[0], one_class, 0)


def marked(slots, rank, cols, mask_ref, first_row, row_count, base, per, keep):
    for j in range(per):
        rank[keep, j] = 0
    total = cols.shape[1]

    def mark(r, _):
        row = jnp.clip(first_row + r, 0, total - 1)
        fits = (first_row + r >= 0) & (first_row + r < total)
        for slot in range(slots):
            local = cols[slot, row] - base

            @pl.when(fits & (mask_ref[slot, row] != 0) & (local >= 0) & (local < per))
            def _():
                rank[keep, jnp.clip(local, 0, per - 1)] = 1

        return 0

    lax.fori_loop(0, row_count, mark, 0)


def level_kernel(plan, ac_ref, ao_ref, am_ref, out_ref, cols, rank):
    slots, a_per, a_rows, a_main = plan
    columns(slots, ac_ref, ao_ref, cols)
    out_ref[0] = 0

    def check(at, _):
        group = at // 4
        first_row = group * a_per + (a_per - a_rows) * lax.rem(at, 2)
        marked(
            slots, rank, cols, am_ref, first_row, a_rows,
            (group - 1 + 2 * lax.rem(at // 2, 2)) * a_per, a_per, 0,
        )
        count = 0
        for j in range(a_per):
            count = count + rank[0, j]

        @pl.when(count > a_main)
        def _():
            out_ref[0] = 1

        return 0

    lax.fori_loop(0, 4 * (cols.shape[1] // a_per), check, 0)


def index_kernel(plan, at_ref, ac_ref, ao_ref, am_ref, bc_ref, bo_ref, bm_ref, out_ref, a_cols, b_cols, rank):
    spots, slots, a_per, a_rows, a_halo, b_per, b_halo = plan
    side, pair, at_ba = at_ref[0], at_ref[1], at_ref[2]
    out_ref[spots.side] = side

    columns(slots, ac_ref, ao_ref, a_cols)
    columns(slots, bc_ref, bo_ref, b_cols)

    def ranked(cols, mask_ref, first_row, row_count, base, per, keep):
        marked(slots, rank, cols, mask_ref, first_row, row_count, base, per, keep)
        count = 0
        for j in range(per):
            used = rank[keep, j]
            rank[keep, j] = count
            count = count + used

    def listed(cols, mask_ref, first_row, row_count, base, per, where, room):
        marked(slots, rank, cols, mask_ref, first_row, row_count, base, per, 2)
        for place in range(room):
            out_ref[where + place] = 0
        count = 0
        for j in range(per):
            used = rank[2, j]

            @pl.when(used != 0)
            def _():
                out_ref[where + jnp.minimum(count, room - 1)] = j

            count = count + used

    def tabled(cols, mask_ref, first_row, row_count, base, per, odd, placed, zero, where):
        def one_row(r, _):
            for slot in range(slots):
                local = cols[slot, first_row + r] - base
                lower = local < 0
                halo = jnp.where(lower, 1 - odd, odd)
                away = jnp.clip(jnp.where(lower, local + per, local - per), 0, per - 1)
                inside = (local >= 0) & (local < per)
                place = placed(inside, local, halo, rank[halo, away])
                live = mask_ref[slot, first_row + r] != 0
                out_ref[where + r * slots + slot] = jnp.where(live, place, zero)
            return 0

        lax.fori_loop(0, row_count, one_row, 0)

    def rows_of(group, at):
        return group * a_per + (a_per - a_rows) * at

    base = pair * a_per
    for which, other in enumerate(partners(pair)):
        listed(a_cols, am_ref, rows_of(other, side), a_rows, base, a_per, spots.a_lists[which], a_halo)
        ranked(a_cols, am_ref, rows_of(pair, side), a_rows, other * a_per, a_per, which)

    def a_placed(inside, local, halo, order):
        return jnp.where(inside, 2 * a_halo + local, halo * a_halo + order)

    tabled(
        a_cols, am_ref, rows_of(pair, side), a_rows, base, a_per, lax.rem(pair, 2), a_placed,
        2 * a_halo + a_per, spots.a_table,
    )
    base = at_ba * b_per
    for which, other in enumerate(partners(at_ba)):
        listed(b_cols, bm_ref, other * b_per, b_per, base, b_per, spots.b_lists[which], b_halo)
        ranked(b_cols, bm_ref, base, b_per, other * b_per, b_per, which)

    def b_placed(inside, local, halo, order):
        return jnp.where(inside, b_halo + local, halo * (b_halo + b_per) + order)

    tabled(
        b_cols, bm_ref, base, b_per, base, b_per, lax.rem(at_ba, 2), b_placed, 2 * b_halo + b_per,
        spots.b_table,
    )


def round_kernel(in_ref, *refs):
    refs[-1][...] = in_ref[...].astype(bf16)


def spot_of(ref, place, blk):
    return pl.ds(pl.multiple_of(ref[place] * blk, blk), blk)


def merge(side, first, keep_ref, recv_ref, into):
    own = keep_ref.shape[0]
    step = 64
    into[pl.ds(pl.multiple_of(first + side * own, step), own), :] = keep_ref[...]
    into[pl.ds(pl.multiple_of(first + (1 - side) * own, step), own), :] = recv_ref[...]


def weights_kernel(first_ref, in_ref, out_ref):
    out_ref[...] = in_ref[...]


def pick_kernel(spots, a_halo, blk, index_ref, keep_ref, recv_ref, *refs):
    whole = refs[-1]
    merge(index_ref[spots.side], 0, keep_ref, recv_ref, whole)
    for which in range(2):
        for place in range(a_halo):
            spot = spot_of(index_ref, spots.a_lists[which] + place, blk)
            refs[which][place * blk : (place + 1) * blk, :] = whole[spot, :]


def alpha_kernel(spots, plan, rounds, index_ref, a_ref, keep_ref, recv_ref, *refs):
    a_per, a_rows, a_halo, blk = plan
    halo_refs, rest_ref = refs[0:2], refs[2]
    ext, term = refs[-2:]
    outs = refs[-4:-2] if rounds else refs[-3:-2]
    side = index_ref[spots.side]
    own = keep_ref.shape[0]
    halo = a_halo * blk
    ext[0:halo, :] = halo_refs[0][...]
    ext[halo : 2 * halo, :] = halo_refs[1][...]
    merge(side, 2 * halo, keep_ref, recv_ref, ext)
    zero = 2 * halo + a_per * blk
    ext[zero : zero + blk, :] = jnp.zeros((blk, ext.shape[1]), ext.dtype)
    slots = a_ref.shape[1]
    for row in range(a_rows):
        parts = [ext[spot_of(index_ref, spots.a_table + row * slots + slot, blk), :] for slot in range(slots)]
        weights = jnp.concatenate([a_ref[row, slot] for slot in range(slots)], axis=1)
        result = jnp.dot(weights, jnp.concatenate(parts, axis=0), preferred_element_type=f32)
        term[row * blk : (row + 1) * blk, :] = result.astype(bf16)
    shift = a_rows * blk - own
    alpha = term[pl.ds(pl.multiple_of(side * shift, 16), own), :].astype(f32)
    newer = rest_ref[...] + 2.0 * alpha
    outs[0][...] = newer
    if rounds:
        outs[1][...] = newer.astype(bf16)


def beta_pick_kernel(spots, b_halo, blk, index_ref, *refs):
    first_ref, second_ref, whole = refs[-3:]
    at = 0
    for chunk in refs[:-3]:
        whole[:, at : at + chunk.shape[1]] = chunk[...]
        at += chunk.shape[1]
    for first, out in zip(spots.b_lists, (first_ref, second_ref)):
        for place in range(b_halo):
            out[:, place * blk : (place + 1) * blk] = whole[:, spot_of(index_ref, first + place, blk)]


def beta_kernel(spots, plan, index_ref, b_ref, *refs):
    b_per, b_halo, blk, wide, count = plan
    low_ref, high_ref, cur_ref, diag_ref, prev_ref = refs[count : count + 5]
    out_ref, ext = refs[-2:]
    step = pl.program_id(0)
    base = b_halo * blk
    top = base + b_per * blk

    @pl.when(step == 0)
    def _():
        ext[:, 0:base] = low_ref[...]
        at = base
        for chunk in refs[:count]:
            ext[:, at : at + chunk.shape[1]] = chunk[...]
            at += chunk.shape[1]
        ext[:, top : top + base] = high_ref[...]
        ext[:, top + base : top + base + blk] = jnp.zeros((ext.shape[0], blk), ext.dtype)

    slots = b_ref.shape[1]
    for one in range(wide):
        first = spots.b_table + (step * wide + one) * slots
        parts = [ext[:, spot_of(index_ref, first + slot, blk)] for slot in range(slots)]
        weights = jnp.concatenate([b_ref[one, slot] for slot in range(slots)], axis=1)
        term = lax.dot_general(
            jnp.concatenate(parts, axis=1), weights, (((1,), (1,)), ((), ())), preferred_element_type=f32
        ).astype(bf16).astype(f32)
        here = slice(one * blk, (one + 1) * blk)
        out_ref[:, here] = 2.0 * (term + diag_ref[:, here] * cur_ref[:, here]) - prev_ref[:, here]


def hbm(x):
    return pltpu.with_memory_space_constraint(x, pltpu.HBM)


def fast(x):
    return pltpu.with_memory_space_constraint(x, VM)


def cost(flops, moved):
    return pl.CostEstimate(flops=flops, bytes_accessed=moved, transcendentals=0)


def limit(mib):
    return pltpu.CompilerParams(vmem_limit_bytes=mib * MIB)


def halo_on_device(
    prev_vector,
    this_vector,
    diagonal,
    alpha_blocks,
    alpha_classes,
    alpha_offsets,
    alpha_mask,
    beta_blocks,
    beta_classes,
    beta_offsets,
    beta_mask,
):
    alpha_count = lax.axis_size("aa")
    beta_count = lax.axis_size("ba")
    own_alpha, own_beta = prev_vector.shape
    row_blocks, slots, blk, _ = alpha_blocks.shape
    a_per = PAIR * own_alpha // blk
    a_rows = -(-own_alpha // blk)
    b_per = own_beta // blk
    a_most = most_needed(A_MOST, slots, (0, a_rows), (-a_per, a_per))
    b_halo = most_needed(B_MOST, slots, (0, b_per), (b_per, b_per))
    parts = [own_beta * share // sum(SHARES) for share in SHARES]
    starts = [sum(parts[:chunk]) for chunk in range(len(parts))]
    chunks = range(len(parts))

    at_aa = lax.axis_index("aa")
    at_ba = lax.axis_index("ba")
    side = at_aa % PAIR
    pair = at_aa // PAIR
    swap = [(i, i ^ 1) for i in range(alpha_count)]
    groups = alpha_count // PAIR

    def swaps(count, first, width):
        both = []
        for low in range(first, count - 1, 2):
            for i in range(width):
                here, there = low * width + i, (low + 1) * width + i
                both += [(here, there), (there, here)]
        return both

    a_ways = [swaps(groups, first, PAIR) for first in range(2)]
    b_ways = [swaps(beta_count, first, 1) for first in range(2)]

    smem = pl.BlockSpec(memory_space=SM)
    vmem = pl.BlockSpec(memory_space=VM)
    free = pl.BlockSpec(memory_space=pl.ANY)

    def shape(rows, columns, dtype=bf16):
        return VM((rows, columns), dtype)

    def tile_of(chunk):
        return 256 if parts[chunk] % 256 == 0 and starts[chunk] % 256 == 0 else 128

    def column(rows, tile, first=0):
        return pl.BlockSpec((rows, tile), lambda g, *_: (0, first + g))

    def rounded(chunk):
        tile = tile_of(chunk)
        return pl.pallas_call(
            round_kernel,
            out_shape=shape(own_alpha, parts[chunk]),
            grid=(parts[chunk] // tile,),
            in_specs=[column(own_alpha, tile, starts[chunk] // tile)],
            out_specs=column(own_alpha, tile),
            compiler_params=limit(6),
            cost_estimate=cost(0, 6 * own_alpha * parts[chunk]),
            name="round",
        )(hbm(this_vector))

    smem_tables = [
        alpha_classes, alpha_offsets.T, alpha_mask.T, beta_classes, beta_offsets.T, beta_mask.T
    ]
    at = jnp.stack([side, pair, at_ba]).astype(i32)
    a_first = jnp.reshape(pair * a_per + side * (a_per - a_rows), (1,)).astype(i32)
    b_first = jnp.reshape(at_ba * b_per, (1,)).astype(i32)

    def body(a_halo):
        spots = Spots(slots, a_rows, a_halo, b_per, b_halo)

        def pick(chunk, keep, recv):
            w, tile = parts[chunk], tile_of(chunk)
            rows = [a_halo * blk] * 2
            return pl.pallas_call(
                functools.partial(pick_kernel, spots, a_halo, blk),
                out_shape=[shape(count, w) for count in rows],
                grid_spec=pltpu.PrefetchScalarGridSpec(
                    num_scalar_prefetch=1,
                    grid=(w // tile,),
                    in_specs=[column(own_alpha, tile)] * 2,
                    out_specs=[column(count, tile) for count in rows],
                    scratch_shapes=[VM((a_per * blk, tile), bf16)],
                ),
                compiler_params=limit(8),
                cost_estimate=cost(0, 2 * (PAIR * own_alpha + 2 * a_halo * blk) * w),
                name="pick",
            )(index, fast(keep), fast(recv))

        def a_halos(picked):
            near = []
            for which in range(2):
                near.append(lax.ppermute(picked[which], "aa", a_ways[which]))
            return near

        def beta_pick(pieces):
            return pl.pallas_call(
                functools.partial(beta_pick_kernel, spots, b_halo, blk),
                out_shape=[shape(own_alpha, b_halo * blk)] * 2,
                in_specs=[smem] + [vmem] * len(pieces),
                out_specs=[vmem, vmem],
                scratch_shapes=[VM((own_alpha, own_beta), bf16)],
                compiler_params=limit(8),
                cost_estimate=cost(0, 4 * own_alpha * own_beta),
                name="beta_pick",
            )(index, *map(fast, pieces))

        wide = 2
        once = pl.Buffered(1)

        def beta(pieces, halos, current, previous):
            strip = pl.BlockSpec((own_alpha, wide * blk), lambda r, index: (0, r))

            def whole(columns):
                return pl.BlockSpec((own_alpha, columns), lambda r, index: (0, 0), pipeline_mode=once)

            return pl.pallas_call(
                functools.partial(beta_kernel, spots, (b_per, b_halo, blk, wide, len(pieces))),
                out_shape=shape(own_alpha, own_beta, f32),
                grid_spec=pltpu.PrefetchScalarGridSpec(
                    num_scalar_prefetch=1,
                    grid=(b_per // wide,),
                    in_specs=[
                        pl.BlockSpec(
                            (wide, slots, blk, blk), lambda r, index: (r, 0, 0, 0)
                        )
                    ]
                    + [whole(part) for part in parts]
                    + [whole(b_halo * blk)] * 2
                    + [strip] * 3
                   ,
                    out_specs=strip,
                    scratch_shapes=[VM((own_alpha, (2 * b_halo + b_per + 1) * blk), bf16)],
                ),
                compiler_params=limit(16),
                cost_estimate=cost(2 * b_per * slots * blk * blk * own_alpha, 16 * own_alpha * own_beta),
                name="beta",
            )(
                index, fast(own_b), *map(fast, pieces), *map(fast, halos), hbm(current), hbm(diagonal), hbm(previous),
            )

        def alpha(chunk, rounds, keep, recv, halos, rest, so_far):
            w, tile = parts[chunk], tile_of(chunk)
            here = column(own_alpha, tile, starts[chunk] // tile)
            operands = [index, *map(fast, (own_a, keep, recv, *halos, rest))]
            in_specs = [pl.BlockSpec((a_rows, slots, blk, blk), lambda g, _: (0, 0, 0, 0))]
            in_specs += [column(own_alpha, tile)] * 2
            in_specs += [column(a_halo * blk, tile)] * 2
            in_specs += [here]
            aliases = {}
            if so_far is not None:
                aliases = {len(operands): 0}
                operands.append(hbm(so_far))
                in_specs.append(free)
            out_shape = [pltpu.HBM((own_alpha, own_beta), f32)]
            out_specs = [here]
            if rounds:
                out_shape.append(shape(own_alpha, w))
                out_specs.append(column(own_alpha, tile))
            return pl.pallas_call(
                functools.partial(alpha_kernel, spots, (a_per, a_rows, a_halo, blk), rounds),
                out_shape=out_shape,
                grid_spec=pltpu.PrefetchScalarGridSpec(
                    num_scalar_prefetch=1,
                    grid=(w // tile,),
                    in_specs=in_specs,
                    out_specs=out_specs,
                    scratch_shapes=[
                        VM(((2 * a_halo + a_per + 1) * blk, tile), bf16),
                        VM((a_rows * blk, tile), bf16),
                    ],
                ),
                input_output_aliases=aliases,
                compiler_params=limit(10),
                cost_estimate=cost(2 * a_rows * slots * blk * blk * w, 16 * own_alpha * w),
                name="alpha",
            )(*operands)

        pieces = []
        for chunk in chunks:
            pieces.append(rounded(chunk))
        index = pl.pallas_call(
            functools.partial(index_kernel, (spots, slots, a_per, a_rows, a_halo, b_per, b_halo)),
            out_shape=jax.ShapeDtypeStruct((spots.size,), i32),
            in_specs=[smem] * 7,
            out_specs=smem,
            scratch_shapes=[
                SM((slots, row_blocks), i32),
                SM((slots, beta_blocks.shape[0]), i32),
                SM((3, max(a_per, b_per)), i32),
            ],
            compiler_params=limit(4),
            cost_estimate=cost(10_000_000, 1_000_000),
            name="index",
        )(at, *smem_tables)

        def weights(blocks, first, count):
            one = (1, slots, blk, blk)
            return pl.pallas_call(
                weights_kernel,
                out_shape=VM((count, slots, blk, blk), bf16),
                grid_spec=pltpu.PrefetchScalarGridSpec(
                    num_scalar_prefetch=1,
                    grid=(count,),
                    in_specs=[pl.BlockSpec(one, lambda g, first: (first[0] + g, 0, 0, 0))],
                    out_specs=pl.BlockSpec(one, lambda g, first: (g, 0, 0, 0)),
                ),
                compiler_params=limit(4),
                cost_estimate=cost(0, 4 * count * slots * blk * blk),
                name="weights",
            )(first, hbm(blocks))

        own_a = weights(alpha_blocks, a_first, a_rows)
        own_b = weights(beta_blocks, b_first, b_per)

        previous, current = prev_vector, this_vector
        produced = []
        for iteration in range(STEPS):
            rounds = iteration < STEPS - 1
            received = []
            for chunk in chunks:
                received.append(lax.ppermute(pieces[chunk], "aa", swap))
            b_picked = beta_pick(pieces)
            b_halos = []
            for which in range(2):
                b_halos.append(lax.ppermute(b_picked[which], "ba", b_ways[which]))
            state = {"newer": None, "fresh": [], "halos": {}}

            def do_beta():
                state["rest"] = beta(pieces, b_halos, current, previous)

            def do_pick(chunk):
                picked = pick(chunk, pieces[chunk], received[chunk])
                state["halos"][chunk] = a_halos(picked)

            def do_alpha(chunk):
                state["newer"], *piece = alpha(
                    chunk, rounds, pieces[chunk], received[chunk], state["halos"][chunk], state["rest"],
                    state["newer"],
                )
                state["fresh"] += piece

            for word in ORDER[iteration]:
                if word == "b":
                    do_beta()
                else:
                    (do_pick if word[0] == "p" else do_alpha)(int(word[1:]))
            pieces = state["fresh"]
            previous, current = current, state["newer"]
            produced.append(current)
        return (produced[0], produced[-1])

    if a_most <= A_MAIN:
        return body(a_most)
    further = pl.pallas_call(
        functools.partial(level_kernel, (slots, a_per, a_rows, A_MAIN)),
        out_shape=jax.ShapeDtypeStruct((1,), i32),
        in_specs=[smem] * 3,
        out_specs=smem,
        scratch_shapes=[SM((slots, row_blocks), i32), SM((1, a_per), i32)],
        compiler_params=limit(4),
        name="level",
    )(*smem_tables[:3])
    return lax.cond(further[0] != 0, lambda: body(a_most), lambda: body(A_MAIN))


def block_columns(class_sizes, offsets):
    class_ends = jnp.cumsum(class_sizes)
    class_starts = class_ends - class_sizes
    row_ids = jnp.arange(offsets.shape[0], dtype=jnp.int32)[:, None]
    inside = (row_ids >= class_starts[None, :]) & (row_ids < class_ends[None, :])
    first_block = jnp.sum(jnp.where(inside, class_starts[None, :], 0), axis=1)
    class_length = jnp.sum(jnp.where(inside, class_sizes[None, :], 0), axis=1)
    return first_block[:, None] + offsets % class_length[:, None]


def couple_last(pieces, blocks, columns, live_mask):
    out_blocks, _, block_size, _ = blocks.shape
    item_count = pieces.shape[0]
    stacked = pieces.reshape(item_count, -1, block_size)
    picked = stacked[:, columns, :] * live_mask[None, :, :, None]
    result = jnp.einsum("crkj,rkij->cri", picked, blocks, preferred_element_type=jnp.float32)
    return result.reshape(item_count, out_blocks * block_size).astype(jnp.bfloat16)


def whole_on_device(
    prev_vector,
    this_vector,
    diagonal,
    alpha_blocks,
    alpha_classes,
    alpha_offsets,
    alpha_mask,
    beta_blocks,
    beta_classes,
    beta_offsets,
    beta_mask,
):
    alpha_cols = block_columns(alpha_classes, alpha_offsets)
    alpha_live = alpha_mask.astype(jnp.bfloat16)
    beta_cols = block_columns(beta_classes, beta_offsets)
    beta_live = beta_mask.astype(jnp.bfloat16)
    alpha_count = lax.axis_size("aa")
    beta_count = lax.axis_size("ba")
    own_alpha, own_beta = prev_vector.shape
    own_count = beta_blocks.shape[0] // beta_count
    first_own = lax.axis_index("ba") * own_count
    own_blocks = lax.dynamic_slice_in_dim(beta_blocks, first_own, own_count, 0)
    own_cols = lax.dynamic_slice_in_dim(beta_cols, first_own, own_count, 0)
    own_live = lax.dynamic_slice_in_dim(beta_live, first_own, own_count, 0)
    previous = prev_vector
    current = this_vector
    produced = []
    for _ in range(STEPS):
        rounded = current.astype(jnp.bfloat16)
        alpha_shaped = rounded.reshape(own_alpha, alpha_count, own_beta // alpha_count)
        pieces = lax.all_to_all(alpha_shaped, "aa", split_axis=1, concat_axis=0, tiled=True)
        whole_alpha, single, columns_here = pieces.shape
        flat = pieces.reshape(whole_alpha, columns_here)
        applied = couple_last(flat.T, alpha_blocks, alpha_cols, alpha_live).T
        alpha_local = applied.reshape(whole_alpha, single, columns_here)
        alpha_back = lax.all_to_all(alpha_local, "aa", split_axis=0, concat_axis=1, tiled=True)
        alpha_term = alpha_back.reshape(own_alpha, own_beta)
        whole_rows = lax.all_gather(rounded, "ba", axis=1, tiled=True)
        beta_term = couple_last(whole_rows, own_blocks, own_cols, own_live)
        newer = (
            2.0
            * (alpha_term.astype(jnp.float32) + beta_term.astype(jnp.float32) + diagonal * current)
            - previous
        )
        previous = current
        current = newer
        produced.append(newer)
    return (produced[0], produced[-1])


def on_device(*args):
    own_alpha, own_beta = args[0].shape
    blk = args[3].shape[-1]
    fits = (
        lax.axis_size("aa") % PAIR == 0
        and (PAIR * own_alpha) % blk == 0
        and PAIR * own_alpha // blk >= A_MOST - 1
        and own_alpha % 64 == 0
        and own_beta % (sum(SHARES) * blk) == 0
        and own_beta // blk >= B_MOST - 1
    )
    return (halo_on_device if fits else whole_on_device)(*args)


def solution(mesh):
    return jax.shard_map(
        on_device,
        mesh=mesh,
        in_specs=(P("aa", "ba"),) * 3 + (P(),) * 8,
        out_specs=(P("aa", "ba"), P("aa", "ba")),
        check_vma=False,
    )
```

```python
import functools

import jax
import jax.numpy as jnp
from jax import lax
from jax.experimental import pallas as pl
from jax.experimental.pallas import tpu as pltpu
from jax.sharding import PartitionSpec as P


STEPS = 2
A_MOST = 8
B_MOST = 10
A_MAIN = 3
B_MAIN = 4
ABSENT = -(1 << 20)
SHARES = (1, 1, 1)
ORDER = (
    ("p0", "b", "a0", "p1", "a1", "p2", "a2"),
    ("p0", "b", "p1", "a0", "p2", "a1", "a2"),
)
PAIR = 2

bf16 = jnp.bfloat16
f32 = jnp.float32
i32 = jnp.int32
VM = pltpu.VMEM
SM = pltpu.SMEM
MIB = 1 << 20


def most_needed(most, slots, rows, blocks):
    best = 0
    for length in range(1, most + 1):
        for start in range(min(rows[0], blocks[0]) - most, max(sum(rows), sum(blocks))):
            held = [
                max(0, min(start + length, sum(part)) - max(start, part[0])) for part in (rows, blocks)
            ]
            best = max(best, min(slots * held[0], held[1]))
    return best


class Spots:
    def __init__(self, slots, a_rows, a_halo, b_per, b_halo):
        self.size = 0
        self.side = self.take(1)
        self.a_lists = [self.take(a_halo + 1), self.take(a_halo + 1)]
        self.a_table = self.take(a_rows * slots)
        self.b_lists = [self.take(b_halo + 1), self.take(b_halo + 1)]
        self.b_table = self.take(b_per * slots)

    def take(self, count):
        first = self.size
        self.size += count
        return first


def partners(group):
    odd = lax.rem(group, 2)
    return group + 1 - 2 * odd, group - 1 + 2 * odd


def columns(slots, most, classes_ref, offsets_ref, mask_ref, cols):
    def one_class(c, start):
        length = classes_ref[c]

        def one_row(r, _):
            for slot in range(slots):
                left = offsets_ref[slot, start + r]
                for bit in reversed(range((most - 1).bit_length())):
                    much = length * (1 << bit)
                    left = jnp.where(left >= much, left - much, left)
                live = mask_ref[slot, start + r] != 0
                cols[slot, start + r] = jnp.where(live, start + left, ABSENT)
            return 0

        lax.fori_loop(0, length, one_row, 0)
        return start + length

    lax.fori_loop(0, classes_ref.shape[0], one_class, 0)


def needed(slots, cols, first_row, row_count, base, per):
    total = cols.shape[1]
    bits = 0
    for r in range(row_count):
        row = first_row + r
        known = isinstance(row, int)
        for slot in range(slots):
            local = cols[slot, row if known else jnp.clip(row, 0, total - 1)] - base
            inside = (local >= 0) & (local < per)
            if not known:
                inside = inside & (row >= 0) & (row < total)
            bits = bits | jnp.where(inside, lax.shift_left(jnp.int32(1), jnp.clip(local, 0, per - 1)), 0)
    return bits


def level_kernel(plan, ac_ref, ao_ref, am_ref, bc_ref, bo_ref, bm_ref, out_ref, a_cols, b_cols):
    slots, a_per, a_rows, a_main, b_per, b_main = plan
    columns(slots, A_MOST, ac_ref, ao_ref, am_ref, a_cols)
    columns(slots, B_MOST, bc_ref, bo_ref, bm_ref, b_cols)
    out_ref[0] = 0

    def check(cols, first_row, row_count, base, per, main):
        bits = needed(slots, cols, first_row, row_count, base, per)
        count = 0
        for j in range(per):
            count = count + (lax.shift_right_logical(bits, j) & 1)

        @pl.when(count > main)
        def _():
            out_ref[0] = 1

    for cols, per, rows, main in ((a_cols, a_per, a_rows, a_main), (b_cols, b_per, b_per, b_main)):
        groups = cols.shape[1] // per
        for group in range(groups):
            for other in (group - 1, group + 1):
                if 0 <= other < groups:
                    for first in sorted({0, per - rows}):
                        check(cols, group * per + first, rows, other * per, per, main)


def partners(group):
    odd = lax.rem(group, 2)
    return group + 1 - 2 * odd, group - 1 + 2 * odd


def index_kernel(plan, at_ref, ac_ref, ao_ref, am_ref, bc_ref, bo_ref, bm_ref, out_ref, a_cols, b_cols, rank):
    spots, slots, a_per, a_rows, a_halo, b_per, b_halo = plan
    side, pair, at_ba = at_ref[0], at_ref[1], at_ref[2]
    out_ref[spots.side] = side
    columns(slots, A_MOST, ac_ref, ao_ref, am_ref, a_cols)
    columns(slots, B_MOST, bc_ref, bo_ref, bm_ref, b_cols)

    def ranked(cols, first_row, row_count, base, per, which):
        bits = needed(slots, cols, first_row, row_count, base, per)
        count = 0
        for j in range(per):
            rank[which, j] = count
            count = count + (lax.shift_right_logical(bits, j) & 1)

    def listed(cols, first_row, row_count, base, per, where, room):
        bits = needed(slots, cols, first_row, row_count, base, per)
        for place in range(room):
            out_ref[where + place] = 0
        count = 0
        for j in range(per):
            out_ref[where + jnp.minimum(count, room)] = j
            count = count + (lax.shift_right_logical(bits, j) & 1)

    def tabled(cols, first_row, row_count, base, per, odd, halo, where):
        for r in range(row_count):
            for slot in range(slots):
                col = cols[slot, first_row + r]
                local = col - base
                lower = local < 0
                which = jnp.where(lower, 1 - odd, odd)
                away = jnp.clip(jnp.where(lower, local + per, local - per), 0, per - 1)
                inside = (local >= 0) & (local < per)
                far = which * halo + jnp.minimum(rank[which, away], halo - 1)
                place = jnp.where(inside, 2 * halo + local, far)
                out_ref[where + r * slots + slot] = jnp.where(col >= 0, place, 2 * halo + per)

    def rows_of(group, at):
        return group * a_per + (a_per - a_rows) * at

    base = pair * a_per
    for which, other in enumerate(partners(pair)):
        listed(a_cols, rows_of(other, side), a_rows, base, a_per, spots.a_lists[which], a_halo)
        ranked(a_cols, rows_of(pair, side), a_rows, other * a_per, a_per, which)
    tabled(a_cols, rows_of(pair, side), a_rows, base, a_per, lax.rem(pair, 2), a_halo, spots.a_table)

    base = at_ba * b_per
    for which, other in enumerate(partners(at_ba)):
        listed(b_cols, other * b_per, b_per, base, b_per, spots.b_lists[which], b_halo)
        ranked(b_cols, base, b_per, other * b_per, b_per, which)
    tabled(b_cols, base, b_per, base, b_per, lax.rem(at_ba, 2), b_halo, spots.b_table)


def round_kernel(in_ref, *refs):
    refs[-1][...] = in_ref[...].astype(bf16)


def spot_of(ref, place, blk):
    return pl.ds(pl.multiple_of(ref[place] * blk, blk), blk)


def merge(side, first, keep_ref, recv_ref, into):
    own = keep_ref.shape[0]
    step = 64
    into[pl.ds(pl.multiple_of(first + side * own, step), own), :] = keep_ref[...]
    into[pl.ds(pl.multiple_of(first + (1 - side) * own, step), own), :] = recv_ref[...]


def weights_kernel(first_ref, in_ref, out_ref):
    out_ref[...] = in_ref[...]


def pick_kernel(spots, a_halo, blk, index_ref, keep_ref, recv_ref, *refs):
    whole = refs[-1]
    merge(index_ref[spots.side], 0, keep_ref, recv_ref, whole)
    for which in range(2):
        for place in range(a_halo):
            spot = spot_of(index_ref, spots.a_lists[which] + place, blk)
            refs[which][place * blk : (place + 1) * blk, :] = whole[spot, :]


def alpha_kernel(spots, plan, rounds, index_ref, a_ref, keep_ref, recv_ref, *refs):
    a_per, a_rows, a_halo, blk = plan
    halo_refs, rest_ref = refs[0:2], refs[2]
    ext, term = refs[-2:]
    outs = refs[-4:-2] if rounds else refs[-3:-2]
    side = index_ref[spots.side]
    own = keep_ref.shape[0]
    halo = a_halo * blk
    ext[0:halo, :] = halo_refs[0][...]
    ext[halo : 2 * halo, :] = halo_refs[1][...]
    merge(side, 2 * halo, keep_ref, recv_ref, ext)
    zero = 2 * halo + a_per * blk
    ext[zero : zero + blk, :] = jnp.zeros((blk, ext.shape[1]), ext.dtype)
    slots = a_ref.shape[1]
    for row in range(a_rows):
        parts = [ext[spot_of(index_ref, spots.a_table + row * slots + slot, blk), :] for slot in range(slots)]
        weights = jnp.concatenate([a_ref[row, slot] for slot in range(slots)], axis=1)
        result = jnp.dot(weights, jnp.concatenate(parts, axis=0), preferred_element_type=f32)
        term[row * blk : (row + 1) * blk, :] = result.astype(bf16)
    shift = a_rows * blk - own
    alpha = term[pl.ds(pl.multiple_of(side * shift, 16), own), :].astype(f32)
    newer = rest_ref[...] + 2.0 * alpha
    outs[0][...] = newer
    if rounds:
        outs[1][...] = newer.astype(bf16)


def beta_pick_kernel(spots, b_halo, blk, index_ref, *refs):
    first_ref, second_ref, whole = refs[-3:]
    at = 0
    for chunk in refs[:-3]:
        whole[:, at : at + chunk.shape[1]] = chunk[...]
        at += chunk.shape[1]
    for first, out in zip(spots.b_lists, (first_ref, second_ref)):
        for place in range(b_halo):
            out[:, place * blk : (place + 1) * blk] = whole[:, spot_of(index_ref, first + place, blk)]


def beta_kernel(spots, plan, index_ref, b_ref, *refs):
    b_per, b_halo, blk, wide, count = plan
    low_ref, high_ref, cur_ref, diag_ref, prev_ref = refs[count : count + 5]
    out_ref, ext = refs[-2:]
    step = pl.program_id(0)
    halo = b_halo * blk
    end = 2 * halo + b_per * blk

    @pl.when(step == 0)
    def _():
        ext[:, 0:halo] = low_ref[...]
        ext[:, halo : 2 * halo] = high_ref[...]
        at = 2 * halo
        for chunk in refs[:count]:
            ext[:, at : at + chunk.shape[1]] = chunk[...]
            at += chunk.shape[1]
        ext[:, end : end + blk] = jnp.zeros((ext.shape[0], blk), ext.dtype)

    slots = b_ref.shape[1]
    for one in range(wide):
        first = spots.b_table + (step * wide + one) * slots
        parts = [ext[:, spot_of(index_ref, first + slot, blk)] for slot in range(slots)]
        weights = jnp.concatenate([b_ref[one, slot] for slot in range(slots)], axis=1)
        term = lax.dot_general(
            jnp.concatenate(parts, axis=1), weights, (((1,), (1,)), ((), ())), preferred_element_type=f32
        ).astype(bf16).astype(f32)
        here = slice(one * blk, (one + 1) * blk)
        out_ref[:, here] = 2.0 * (term + diag_ref[:, here] * cur_ref[:, here]) - prev_ref[:, here]


def hbm(x):
    return pltpu.with_memory_space_constraint(x, pltpu.HBM)


def fast(x):
    return pltpu.with_memory_space_constraint(x, VM)


def cost(flops, moved):
    return pl.CostEstimate(flops=flops, bytes_accessed=moved, transcendentals=0)


def limit(mib):
    return pltpu.CompilerParams(vmem_limit_bytes=mib * MIB)


def halo_on_device(
    prev_vector,
    this_vector,
    diagonal,
    alpha_blocks,
    alpha_classes,
    alpha_offsets,
    alpha_mask,
    beta_blocks,
    beta_classes,
    beta_offsets,
    beta_mask,
):
    alpha_count = lax.axis_size("aa")
    beta_count = lax.axis_size("ba")
    own_alpha, own_beta = prev_vector.shape
    row_blocks, slots, blk, _ = alpha_blocks.shape
    a_per = PAIR * own_alpha // blk
    a_rows = -(-own_alpha // blk)
    b_per = own_beta // blk
    a_most = most_needed(A_MOST, slots, (0, a_rows), (-a_per, a_per))
    b_most = most_needed(B_MOST, slots, (0, b_per), (b_per, b_per))
    parts = [own_beta * share // sum(SHARES) for share in SHARES]
    starts = [sum(parts[:chunk]) for chunk in range(len(parts))]
    chunks = range(len(parts))

    at_aa = lax.axis_index("aa")
    at_ba = lax.axis_index("ba")
    side = at_aa % PAIR
    pair = at_aa // PAIR
    swap = [(i, i ^ 1) for i in range(alpha_count)]
    groups = alpha_count // PAIR

    def swaps(count, first, width):
        both = []
        for low in range(first, count - 1, 2):
            for i in range(width):
                here, there = low * width + i, (low + 1) * width + i
                both += [(here, there), (there, here)]
        return both

    a_ways = []
    for first in range(2):
        both = dict(swaps(groups, first, PAIR))
        way = []
        for i in range(alpha_count):
            for j in range(beta_count):
                there = (both[i], j) if i in both else (i, j ^ 1)
                way.append((i * beta_count + j, there[0] * beta_count + there[1]))
        a_ways.append(way)
    b_ways = [swaps(beta_count, first, 1) for first in range(2)]

    smem = pl.BlockSpec(memory_space=SM)
    vmem = pl.BlockSpec(memory_space=VM)
    free = pl.BlockSpec(memory_space=pl.ANY)

    def shape(rows, columns, dtype=bf16):
        return VM((rows, columns), dtype)

    def tile_of(chunk):
        return 256 if parts[chunk] % 256 == 0 and starts[chunk] % 256 == 0 else 128

    def column(rows, tile, first=0):
        return pl.BlockSpec((rows, tile), lambda g, *_: (0, first + g))

    def rounded(chunk):
        tile = tile_of(chunk)
        return pl.pallas_call(
            round_kernel,
            out_shape=shape(own_alpha, parts[chunk]),
            grid=(parts[chunk] // tile,),
            in_specs=[column(own_alpha, tile, starts[chunk] // tile)],
            out_specs=column(own_alpha, tile),
            compiler_params=limit(6),
            cost_estimate=cost(0, 6 * own_alpha * parts[chunk]),
            name="round",
        )(hbm(this_vector))

    smem_tables = [
        alpha_classes, alpha_offsets.T, alpha_mask.T, beta_classes, beta_offsets.T, beta_mask.T
    ]
    at = jnp.stack([side, pair, at_ba]).astype(i32)
    a_first = jnp.reshape(pair * a_per + side * (a_per - a_rows), (1,)).astype(i32)
    b_first = jnp.reshape(at_ba, (1,)).astype(i32)

    def body(a_halo, b_halo):
        spots = Spots(slots, a_rows, a_halo, b_per, b_halo)

        def pick(chunk, keep, recv):
            w, tile = parts[chunk], tile_of(chunk)
            rows = [a_halo * blk] * 2
            return pl.pallas_call(
                functools.partial(pick_kernel, spots, a_halo, blk),
                out_shape=[shape(count, w) for count in rows],
                grid_spec=pltpu.PrefetchScalarGridSpec(
                    num_scalar_prefetch=1,
                    grid=(w // tile,),
                    in_specs=[column(own_alpha, tile)] * 2,
                    out_specs=[column(count, tile) for count in rows],
                    scratch_shapes=[VM((a_per * blk, tile), bf16)],
                ),
                compiler_params=limit(8),
                cost_estimate=cost(0, 2 * (PAIR * own_alpha + 2 * a_halo * blk) * w),
                name="pick",
            )(index, fast(keep), fast(recv))

        def a_halos(picked):
            near = []
            for which in range(2):
                near.append(lax.ppermute(picked[which], ("aa", "ba"), a_ways[which]))
            return near

        def beta_pick(pieces):
            return pl.pallas_call(
                functools.partial(beta_pick_kernel, spots, b_halo, blk),
                out_shape=[shape(own_alpha, b_halo * blk)] * 2,
                in_specs=[smem] + [vmem] * len(pieces),
                out_specs=[vmem, vmem],
                scratch_shapes=[VM((own_alpha, own_beta), bf16)],
                compiler_params=limit(8),
                cost_estimate=cost(0, 4 * own_alpha * own_beta),
                name="beta_pick",
            )(index, *map(fast, pieces))

        wide = 2
        once = pl.Buffered(1)

        def beta(own_b, pieces, halos, current, previous):
            strip = pl.BlockSpec((own_alpha, wide * blk), lambda r, index: (0, r))

            def whole(columns):
                return pl.BlockSpec((own_alpha, columns), lambda r, index: (0, 0), pipeline_mode=once)

            return pl.pallas_call(
                functools.partial(beta_kernel, spots, (b_per, b_halo, blk, wide, len(pieces))),
                out_shape=shape(own_alpha, own_beta, f32),
                grid_spec=pltpu.PrefetchScalarGridSpec(
                    num_scalar_prefetch=1,
                    grid=(b_per // wide,),
                    in_specs=[
                        pl.BlockSpec(
                            (wide, slots, blk, blk), lambda r, index: (r, 0, 0, 0)
                        )
                    ]
                    + [whole(part) for part in parts]
                    + [whole(b_halo * blk)] * 2
                    + [strip] * 3
                   ,
                    out_specs=strip,
                    scratch_shapes=[VM((own_alpha, (2 * b_halo + b_per + 1) * blk), bf16)],
                ),
                compiler_params=limit(16),
                cost_estimate=cost(2 * b_per * slots * blk * blk * own_alpha, 16 * own_alpha * own_beta),
                name="beta",
            )(
                index, fast(own_b), *map(fast, pieces), *map(fast, halos), hbm(current), hbm(diagonal), hbm(previous),
            )

        def alpha(own_a, chunk, rounds, keep, recv, halos, rest, so_far):
            w, tile = parts[chunk], tile_of(chunk)
            here = column(own_alpha, tile, starts[chunk] // tile)
            operands = [index, *map(fast, (own_a, keep, recv, *halos, rest))]
            in_specs = [pl.BlockSpec((a_rows, slots, blk, blk), lambda g, _: (0, 0, 0, 0))]
            in_specs += [column(own_alpha, tile)] * 2
            in_specs += [column(a_halo * blk, tile)] * 2
            in_specs += [here]
            aliases = {}
            if so_far is not None:
                aliases = {len(operands): 0}
                operands.append(hbm(so_far))
                in_specs.append(free)
            out_shape = [pltpu.HBM((own_alpha, own_beta), f32)]
            out_specs = [here]
            if rounds:
                out_shape.append(shape(own_alpha, w))
                out_specs.append(column(own_alpha, tile))
            return pl.pallas_call(
                functools.partial(alpha_kernel, spots, (a_per, a_rows, a_halo, blk), rounds),
                out_shape=out_shape,
                grid_spec=pltpu.PrefetchScalarGridSpec(
                    num_scalar_prefetch=1,
                    grid=(w // tile,),
                    in_specs=in_specs,
                    out_specs=out_specs,
                    scratch_shapes=[
                        VM(((2 * a_halo + a_per + 1) * blk, tile), bf16),
                        VM((a_rows * blk, tile), bf16),
                    ],
                ),
                input_output_aliases=aliases,
                compiler_params=limit(10),
                cost_estimate=cost(2 * a_rows * slots * blk * blk * w, 16 * own_alpha * w),
                name="alpha",
            )(*operands)

        pieces = []
        for chunk in chunks:
            pieces.append(rounded(chunk))
        index = pl.pallas_call(
            functools.partial(index_kernel, (spots, slots, a_per, a_rows, a_halo, b_per, b_halo)),
            out_shape=jax.ShapeDtypeStruct((spots.size,), i32),
            in_specs=[smem] * 7,
            out_specs=smem,
            scratch_shapes=[
                SM((slots, row_blocks), i32),
                SM((slots, beta_blocks.shape[0]), i32),
                SM((2, max(a_per, b_per)), i32),
            ],
            compiler_params=limit(4),
            cost_estimate=cost(10_000_000, 1_000_000),
            name="index",
        )(at, *smem_tables)

        def weights(blocks, first, count, at_once):
            one = (at_once, slots, blk, blk)
            return pl.pallas_call(
                weights_kernel,
                out_shape=VM((count, slots, blk, blk), bf16),
                grid_spec=pltpu.PrefetchScalarGridSpec(
                    num_scalar_prefetch=1,
                    grid=(count // at_once,),
                    in_specs=[pl.BlockSpec(one, lambda g, first: (first[0] + g, 0, 0, 0))],
                    out_specs=pl.BlockSpec(one, lambda g, first: (g, 0, 0, 0)),
                ),
                compiler_params=limit(4),
                cost_estimate=cost(0, 4 * count * slots * blk * blk),
                name="weights",
            )(first, hbm(blocks))

        previous, current = prev_vector, this_vector
        produced = []
        for iteration in range(STEPS):
            rounds = iteration < STEPS - 1
            received = []
            for chunk in chunks:
                received.append(lax.ppermute(pieces[chunk], "aa", swap))
            b_picked = beta_pick(pieces)
            b_halos = []
            for which in range(2):
                b_halos.append(lax.ppermute(b_picked[which], "ba", b_ways[which]))
            if iteration == 0:
                own_a = weights(alpha_blocks, a_first, a_rows, 1)
                own_b = weights(beta_blocks, b_first, b_per, b_per)
            state = {"newer": None, "fresh": [], "halos": {}}

            def do_beta():
                state["rest"] = beta(own_b, pieces, b_halos, current, previous)

            def do_pick(chunk):
                picked = pick(chunk, pieces[chunk], received[chunk])
                state["halos"][chunk] = a_halos(picked)

            def do_alpha(chunk):
                state["newer"], *piece = alpha(
                    own_a, chunk, rounds, pieces[chunk], received[chunk], state["halos"][chunk], state["rest"],
                    state["newer"],
                )
                state["fresh"] += piece

            for word in ORDER[iteration]:
                if word == "b":
                    do_beta()
                else:
                    (do_pick if word[0] == "p" else do_alpha)(int(word[1:]))
            pieces = state["fresh"]
            previous, current = current, state["newer"]
            produced.append(current)
        return (produced[0], produced[-1])

    if a_most <= A_MAIN and b_most <= B_MAIN:
        return body(a_most, b_most)
    further = pl.pallas_call(
        functools.partial(level_kernel, (slots, a_per, a_rows, A_MAIN, b_per, B_MAIN)),
        out_shape=jax.ShapeDtypeStruct((1,), i32),
        in_specs=[smem] * 6,
        out_specs=smem,
        scratch_shapes=[SM((slots, row_blocks), i32), SM((slots, beta_blocks.shape[0]), i32)],
        compiler_params=limit(4),
        name="level",
    )(*smem_tables)
    return lax.cond(
        further[0] != 0, lambda: body(a_most, b_most), lambda: body(min(a_most, A_MAIN), min(b_most, B_MAIN))
    )


def block_columns(class_sizes, offsets):
    class_ends = jnp.cumsum(class_sizes)
    class_starts = class_ends - class_sizes
    row_ids = jnp.arange(offsets.shape[0], dtype=jnp.int32)[:, None]
    inside = (row_ids >= class_starts[None, :]) & (row_ids < class_ends[None, :])
    first_block = jnp.sum(jnp.where(inside, class_starts[None, :], 0), axis=1)
    class_length = jnp.sum(jnp.where(inside, class_sizes[None, :], 0), axis=1)
    return first_block[:, None] + offsets % class_length[:, None]


def couple_last(pieces, blocks, columns, live_mask):
    out_blocks, _, block_size, _ = blocks.shape
    item_count = pieces.shape[0]
    stacked = pieces.reshape(item_count, -1, block_size)
    picked = stacked[:, columns, :] * live_mask[None, :, :, None]
    result = jnp.einsum("crkj,rkij->cri", picked, blocks, preferred_element_type=jnp.float32)
    return result.reshape(item_count, out_blocks * block_size).astype(jnp.bfloat16)


def whole_on_device(
    prev_vector,
    this_vector,
    diagonal,
    alpha_blocks,
    alpha_classes,
    alpha_offsets,
    alpha_mask,
    beta_blocks,
    beta_classes,
    beta_offsets,
    beta_mask,
):
    alpha_cols = block_columns(alpha_classes, alpha_offsets)
    alpha_live = alpha_mask.astype(jnp.bfloat16)
    beta_cols = block_columns(beta_classes, beta_offsets)
    beta_live = beta_mask.astype(jnp.bfloat16)
    alpha_count = lax.axis_size("aa")
    beta_count = lax.axis_size("ba")
    own_alpha, own_beta = prev_vector.shape
    own_count = beta_blocks.shape[0] // beta_count
    first_own = lax.axis_index("ba") * own_count
    own_blocks = lax.dynamic_slice_in_dim(beta_blocks, first_own, own_count, 0)
    own_cols = lax.dynamic_slice_in_dim(beta_cols, first_own, own_count, 0)
    own_live = lax.dynamic_slice_in_dim(beta_live, first_own, own_count, 0)
    previous = prev_vector
    current = this_vector
    produced = []
    for _ in range(STEPS):
        rounded = current.astype(jnp.bfloat16)
        alpha_shaped = rounded.reshape(own_alpha, alpha_count, own_beta // alpha_count)
        pieces = lax.all_to_all(alpha_shaped, "aa", split_axis=1, concat_axis=0, tiled=True)
        whole_alpha, single, columns_here = pieces.shape
        flat = pieces.reshape(whole_alpha, columns_here)
        applied = couple_last(flat.T, alpha_blocks, alpha_cols, alpha_live).T
        alpha_local = applied.reshape(whole_alpha, single, columns_here)
        alpha_back = lax.all_to_all(alpha_local, "aa", split_axis=0, concat_axis=1, tiled=True)
        alpha_term = alpha_back.reshape(own_alpha, own_beta)
        whole_rows = lax.all_gather(rounded, "ba", axis=1, tiled=True)
        beta_term = couple_last(whole_rows, own_blocks, own_cols, own_live)
        newer = (
            2.0
            * (alpha_term.astype(jnp.float32) + beta_term.astype(jnp.float32) + diagonal * current)
            - previous
        )
        previous = current
        current = newer
        produced.append(newer)
    return (produced[0], produced[-1])


def on_device(*args):
    own_alpha, own_beta = args[0].shape
    blk = args[3].shape[-1]
    fits = (
        lax.axis_size("aa") % PAIR == 0
        and (PAIR * own_alpha) % blk == 0
        and PAIR * own_alpha // blk >= A_MOST - 1
        and own_alpha % 64 == 0
        and own_beta % (sum(SHARES) * blk) == 0
        and own_beta // blk >= B_MOST - 1
        and lax.axis_size("ba") % 2 == 0
    )
    return (halo_on_device if fits else whole_on_device)(*args)


def solution(mesh):
    return jax.shard_map(
        on_device,
        mesh=mesh,
        in_specs=(P("aa", "ba"),) * 3 + (P(),) * 8,
        out_specs=(P("aa", "ba"), P("aa", "ba")),
        check_vma=False,
    )
```

```python
import functools

import jax
import jax.numpy as jnp
from jax import lax
from jax.experimental import pallas as pl
from jax.experimental.pallas import tpu as pltpu
from jax.sharding import PartitionSpec as P


STEPS = 2
A_MOST = 8
B_MOST = 10
A_MAIN = 3
B_MAIN = 4
ABSENT = -(1 << 20)
SHARES = (1, 1, 1)
ORDER = (
    "q0", "w0", "w1", "p00", "b0", "a00", "p01", "p02",
    "a01", "p10", "a02", "q1", "p11", "b1", "a10", "p12",
    "a11", "a12",
)
PAIR = 2

bf16 = jnp.bfloat16
f32 = jnp.float32
i32 = jnp.int32
VM = pltpu.VMEM
SM = pltpu.SMEM
MIB = 1 << 20


def most_needed(most, slots, rows, blocks):
    best = 0
    for length in range(1, most + 1):
        for start in range(min(rows[0], blocks[0]) - most, max(sum(rows), sum(blocks))):
            held = [
                max(0, min(start + length, sum(part)) - max(start, part[0])) for part in (rows, blocks)
            ]
            best = max(best, min(slots * held[0], held[1]))
    return best


class Spots:
    def __init__(self, slots, a_rows, a_halo, b_per, b_halo):
        self.size = 0
        self.side = self.take(1)
        self.a_lists = [self.take(a_halo + 1), self.take(a_halo + 1)]
        self.a_table = self.take(a_rows * slots)
        self.b_lists = [self.take(b_halo + 1), self.take(b_halo + 1)]
        self.b_table = self.take(b_per * slots)

    def take(self, count):
        first = self.size
        self.size += count
        return first


def partners(group):
    odd = lax.rem(group, 2)
    return group + 1 - 2 * odd, group - 1 + 2 * odd


def columns(slots, most, classes_ref, offsets_ref, mask_ref, cols):
    last = classes_ref.shape[0] - 1
    which, start, length = jnp.int32(0), jnp.int32(0), classes_ref[0]
    for row in range(cols.shape[1]):
        if row:
            over = row >= start + length
            which = jnp.where(over, jnp.minimum(which + 1, last), which)
            start = jnp.where(over, row, start)
            length = classes_ref[which]
        for slot in range(slots):
            left = offsets_ref[slot, row]
            for bit in reversed(range((most - 1).bit_length())):
                much = length * (1 << bit)
                left = jnp.where(left >= much, left - much, left)
            cols[slot, row] = jnp.where(mask_ref[slot, row] != 0, start + left, ABSENT)


def needed(slots, cols, first_row, row_count, base, per):
    total = cols.shape[1]
    bits = 0
    for r in range(row_count):
        row = first_row + r
        known = isinstance(row, int)
        for slot in range(slots):
            local = cols[slot, row if known else jnp.clip(row, 0, total - 1)] - base
            inside = (local >= 0) & (local < per)
            if not known:
                inside = inside & (row >= 0) & (row < total)
            bits = bits | jnp.where(inside, lax.shift_left(jnp.int32(1), jnp.clip(local, 0, per - 1)), 0)
    return bits


def level_kernel(plan, ac_ref, ao_ref, am_ref, bc_ref, bo_ref, bm_ref, out_ref, a_cols, b_cols):
    slots, a_per, a_rows, a_main, b_per, b_main = plan
    columns(slots, A_MOST, ac_ref, ao_ref, am_ref, a_cols)
    columns(slots, B_MOST, bc_ref, bo_ref, bm_ref, b_cols)
    out_ref[0] = 0

    def check(cols, first_row, row_count, base, per, main):
        bits = needed(slots, cols, first_row, row_count, base, per)
        count = 0
        for j in range(per):
            count = count + (lax.shift_right_logical(bits, j) & 1)

        @pl.when(count > main)
        def _():
            out_ref[0] = 1

    for cols, per, rows, main in ((a_cols, a_per, a_rows, a_main), (b_cols, b_per, b_per, b_main)):
        groups = cols.shape[1] // per
        for group in range(groups):
            for other in (group - 1, group + 1):
                if 0 <= other < groups:
                    for first in sorted({0, per - rows}):
                        check(cols, group * per + first, rows, other * per, per, main)


def partners(group):
    odd = lax.rem(group, 2)
    return group + 1 - 2 * odd, group - 1 + 2 * odd


def index_kernel(plan, at_ref, ac_ref, ao_ref, am_ref, bc_ref, bo_ref, bm_ref, out_ref, a_cols, b_cols, rank):
    spots, slots, a_per, a_rows, a_halo, b_per, b_halo = plan
    side, pair, at_ba = at_ref[0], at_ref[1], at_ref[2]
    out_ref[spots.side] = side
    columns(slots, A_MOST, ac_ref, ao_ref, am_ref, a_cols)
    columns(slots, B_MOST, bc_ref, bo_ref, bm_ref, b_cols)

    def ranked(cols, first_row, row_count, base, per, which):
        bits = needed(slots, cols, first_row, row_count, base, per)
        count = 0
        for j in range(per):
            rank[which, j] = count
            count = count + (lax.shift_right_logical(bits, j) & 1)

    def listed(cols, first_row, row_count, base, per, where, room):
        bits = needed(slots, cols, first_row, row_count, base, per)
        for place in range(room):
            out_ref[where + place] = 0
        count = 0
        for j in range(per):
            out_ref[where + jnp.minimum(count, room)] = j
            count = count + (lax.shift_right_logical(bits, j) & 1)

    def tabled(cols, first_row, row_count, base, per, odd, halo, where):
        for r in range(row_count):
            for slot in range(slots):
                col = cols[slot, first_row + r]
                local = col - base
                lower = local < 0
                which = jnp.where(lower, 1 - odd, odd)
                away = jnp.clip(jnp.where(lower, local + per, local - per), 0, per - 1)
                inside = (local >= 0) & (local < per)
                far = which * halo + jnp.minimum(rank[which, away], halo - 1)
                place = jnp.where(inside, 2 * halo + local, far)
                out_ref[where + r * slots + slot] = jnp.where(col >= 0, place, 2 * halo + per)

    def rows_of(group, at):
        return group * a_per + (a_per - a_rows) * at

    base = pair * a_per
    for which, other in enumerate(partners(pair)):
        listed(a_cols, rows_of(other, side), a_rows, base, a_per, spots.a_lists[which], a_halo)
        ranked(a_cols, rows_of(pair, side), a_rows, other * a_per, a_per, which)
    tabled(a_cols, rows_of(pair, side), a_rows, base, a_per, lax.rem(pair, 2), a_halo, spots.a_table)

    base = at_ba * b_per
    for which, other in enumerate(partners(at_ba)):
        listed(b_cols, other * b_per, b_per, base, b_per, spots.b_lists[which], b_halo)
        ranked(b_cols, base, b_per, other * b_per, b_per, which)
    tabled(b_cols, base, b_per, base, b_per, lax.rem(at_ba, 2), b_halo, spots.b_table)


def round_kernel(in_ref, *refs):
    refs[-1][...] = in_ref[...].astype(bf16)


def spot_of(ref, place, blk):
    return pl.ds(pl.multiple_of(ref[place] * blk, blk), blk)


def merge(side, first, keep_ref, recv_ref, into):
    own = keep_ref.shape[0]
    step = 64
    into[pl.ds(pl.multiple_of(first + side * own, step), own), :] = keep_ref[...]
    into[pl.ds(pl.multiple_of(first + (1 - side) * own, step), own), :] = recv_ref[...]


def weights_kernel(first_ref, in_ref, out_ref):
    out_ref[...] = in_ref[...]


def pick_kernel(spots, a_halo, blk, index_ref, keep_ref, recv_ref, *refs):
    whole = refs[-1]
    merge(index_ref[spots.side], 0, keep_ref, recv_ref, whole)
    for which in range(2):
        for place in range(a_halo):
            spot = spot_of(index_ref, spots.a_lists[which] + place, blk)
            refs[which][place * blk : (place + 1) * blk, :] = whole[spot, :]


def alpha_kernel(spots, plan, rounds, index_ref, a_ref, keep_ref, recv_ref, *refs):
    a_per, a_rows, a_halo, blk = plan
    halo_refs, rest_ref = refs[0:2], refs[2]
    ext, term = refs[-2:]
    outs = refs[-4:-2] if rounds else refs[-3:-2]
    side = index_ref[spots.side]
    own = keep_ref.shape[0]
    halo = a_halo * blk
    ext[0:halo, :] = halo_refs[0][...]
    ext[halo : 2 * halo, :] = halo_refs[1][...]
    merge(side, 2 * halo, keep_ref, recv_ref, ext)
    zero = 2 * halo + a_per * blk
    ext[zero : zero + blk, :] = jnp.zeros((blk, ext.shape[1]), ext.dtype)
    slots = a_ref.shape[1]
    for row in range(a_rows):
        parts = [ext[spot_of(index_ref, spots.a_table + row * slots + slot, blk), :] for slot in range(slots)]
        weights = jnp.concatenate([a_ref[row, slot] for slot in range(slots)], axis=1)
        result = jnp.dot(weights, jnp.concatenate(parts, axis=0), preferred_element_type=f32)
        term[row * blk : (row + 1) * blk, :] = result.astype(bf16)
    shift = a_rows * blk - own
    alpha = term[pl.ds(pl.multiple_of(side * shift, 16), own), :].astype(f32)
    newer = rest_ref[...] + 2.0 * alpha
    outs[0][...] = newer
    if rounds:
        outs[1][...] = newer.astype(bf16)


def beta_pick_kernel(spots, b_halo, blk, index_ref, *refs):
    first_ref, second_ref, whole = refs[-3:]
    at = 0
    for chunk in refs[:-3]:
        whole[:, at : at + chunk.shape[1]] = chunk[...]
        at += chunk.shape[1]
    for first, out in zip(spots.b_lists, (first_ref, second_ref)):
        for place in range(b_halo):
            out[:, place * blk : (place + 1) * blk] = whole[:, spot_of(index_ref, first + place, blk)]


def beta_kernel(spots, plan, index_ref, b_ref, *refs):
    b_per, b_halo, blk, wide, count = plan
    low_ref, high_ref, cur_ref, diag_ref, prev_ref = refs[count : count + 5]
    out_ref, ext = refs[-2:]
    step = pl.program_id(0)
    halo = b_halo * blk
    end = 2 * halo + b_per * blk

    @pl.when(step == 0)
    def _():
        ext[:, 0:halo] = low_ref[...]
        ext[:, halo : 2 * halo] = high_ref[...]
        at = 2 * halo
        for chunk in refs[:count]:
            ext[:, at : at + chunk.shape[1]] = chunk[...]
            at += chunk.shape[1]
        ext[:, end : end + blk] = jnp.zeros((ext.shape[0], blk), ext.dtype)

    slots = b_ref.shape[1]
    for one in range(wide):
        first = spots.b_table + (step * wide + one) * slots
        parts = [ext[:, spot_of(index_ref, first + slot, blk)] for slot in range(slots)]
        weights = jnp.concatenate([b_ref[one, slot] for slot in range(slots)], axis=1)
        term = lax.dot_general(
            jnp.concatenate(parts, axis=1), weights, (((1,), (1,)), ((), ())), preferred_element_type=f32
        ).astype(bf16).astype(f32)
        here = slice(one * blk, (one + 1) * blk)
        out_ref[:, here] = 2.0 * (term + diag_ref[:, here] * cur_ref[:, here]) - prev_ref[:, here]


def hbm(x):
    return pltpu.with_memory_space_constraint(x, pltpu.HBM)


def fast(x):
    return pltpu.with_memory_space_constraint(x, VM)


def cost(flops, moved):
    return pl.CostEstimate(flops=flops, bytes_accessed=moved, transcendentals=0)


def limit(mib):
    return pltpu.CompilerParams(vmem_limit_bytes=mib * MIB)


def halo_on_device(
    prev_vector,
    this_vector,
    diagonal,
    alpha_blocks,
    alpha_classes,
    alpha_offsets,
    alpha_mask,
    beta_blocks,
    beta_classes,
    beta_offsets,
    beta_mask,
):
    alpha_count = lax.axis_size("aa")
    beta_count = lax.axis_size("ba")
    own_alpha, own_beta = prev_vector.shape
    row_blocks, slots, blk, _ = alpha_blocks.shape
    a_per = PAIR * own_alpha // blk
    a_rows = -(-own_alpha // blk)
    b_per = own_beta // blk
    a_most = most_needed(A_MOST, slots, (0, a_rows), (-a_per, a_per))
    b_most = most_needed(B_MOST, slots, (0, b_per), (b_per, b_per))
    parts = [own_beta * share // sum(SHARES) for share in SHARES]
    starts = [sum(parts[:chunk]) for chunk in range(len(parts))]
    chunks = range(len(parts))

    at_aa = lax.axis_index("aa")
    at_ba = lax.axis_index("ba")
    side = at_aa % PAIR
    pair = at_aa // PAIR
    swap = [(i, i ^ 1) for i in range(alpha_count)]
    groups = alpha_count // PAIR

    def swaps(count, first, width):
        both = []
        for low in range(first, count - 1, 2):
            for i in range(width):
                here, there = low * width + i, (low + 1) * width + i
                both += [(here, there), (there, here)]
        return both

    a_ways = []
    for first in range(2):
        both = dict(swaps(groups, first, PAIR))
        way = []
        for i in range(alpha_count):
            for j in range(beta_count):
                there = (both[i], j) if i in both else (i, j ^ 1)
                way.append((i * beta_count + j, there[0] * beta_count + there[1]))
        a_ways.append(way)
    b_ways = [swaps(beta_count, first, 1) for first in range(2)]

    smem = pl.BlockSpec(memory_space=SM)
    vmem = pl.BlockSpec(memory_space=VM)
    free = pl.BlockSpec(memory_space=pl.ANY)

    def shape(rows, columns, dtype=bf16):
        return VM((rows, columns), dtype)

    def tile_of(chunk):
        return 256 if parts[chunk] % 256 == 0 and starts[chunk] % 256 == 0 else 128

    def column(rows, tile, first=0):
        return pl.BlockSpec((rows, tile), lambda g, *_: (0, first + g))

    def rounded(chunk):
        tile = tile_of(chunk)
        return pl.pallas_call(
            round_kernel,
            out_shape=shape(own_alpha, parts[chunk]),
            grid=(parts[chunk] // tile,),
            in_specs=[column(own_alpha, tile, starts[chunk] // tile)],
            out_specs=column(own_alpha, tile),
            compiler_params=limit(6),
            cost_estimate=cost(0, 6 * own_alpha * parts[chunk]),
            name="round",
        )(hbm(this_vector))

    smem_tables = [
        alpha_classes, alpha_offsets.T, alpha_mask.T, beta_classes, beta_offsets.T, beta_mask.T
    ]
    at = jnp.stack([side, pair, at_ba]).astype(i32)
    a_first = jnp.reshape(pair * a_per + side * (a_per - a_rows), (1,)).astype(i32)
    b_first = jnp.reshape(at_ba, (1,)).astype(i32)

    def body(a_halo, b_halo):
        spots = Spots(slots, a_rows, a_halo, b_per, b_halo)

        def pick(chunk, keep, recv):
            w, tile = parts[chunk], tile_of(chunk)
            rows = [a_halo * blk] * 2
            return pl.pallas_call(
                functools.partial(pick_kernel, spots, a_halo, blk),
                out_shape=[shape(count, w) for count in rows],
                grid_spec=pltpu.PrefetchScalarGridSpec(
                    num_scalar_prefetch=1,
                    grid=(w // tile,),
                    in_specs=[column(own_alpha, tile)] * 2,
                    out_specs=[column(count, tile) for count in rows],
                    scratch_shapes=[VM((a_per * blk, tile), bf16)],
                ),
                compiler_params=limit(8),
                cost_estimate=cost(0, 2 * (PAIR * own_alpha + 2 * a_halo * blk) * w),
                name="pick",
            )(index, fast(keep), fast(recv))

        def a_halos(picked):
            near = []
            for which in range(2):
                near.append(lax.ppermute(picked[which], ("aa", "ba"), a_ways[which]))
            return near

        def beta_pick(pieces):
            return pl.pallas_call(
                functools.partial(beta_pick_kernel, spots, b_halo, blk),
                out_shape=[shape(own_alpha, b_halo * blk)] * 2,
                in_specs=[smem] + [vmem] * len(pieces),
                out_specs=[vmem, vmem],
                scratch_shapes=[VM((own_alpha, own_beta), bf16)],
                compiler_params=limit(8),
                cost_estimate=cost(0, 4 * own_alpha * own_beta),
                name="beta_pick",
            )(index, *map(fast, pieces))

        wide = 2
        once = pl.Buffered(1)

        def beta(own_b, pieces, halos, current, previous):
            strip = pl.BlockSpec((own_alpha, wide * blk), lambda r, index: (0, r))

            def whole(columns):
                return pl.BlockSpec((own_alpha, columns), lambda r, index: (0, 0), pipeline_mode=once)

            return pl.pallas_call(
                functools.partial(beta_kernel, spots, (b_per, b_halo, blk, wide, len(pieces))),
                out_shape=shape(own_alpha, own_beta, f32),
                grid_spec=pltpu.PrefetchScalarGridSpec(
                    num_scalar_prefetch=1,
                    grid=(b_per // wide,),
                    in_specs=[
                        pl.BlockSpec(
                            (wide, slots, blk, blk), lambda r, index: (r, 0, 0, 0)
                        )
                    ]
                    + [whole(part) for part in parts]
                    + [whole(b_halo * blk)] * 2
                    + [strip] * 3
                   ,
                    out_specs=strip,
                    scratch_shapes=[VM((own_alpha, (2 * b_halo + b_per + 1) * blk), bf16)],
                ),
                compiler_params=limit(16),
                cost_estimate=cost(2 * b_per * slots * blk * blk * own_alpha, 16 * own_alpha * own_beta),
                name="beta",
            )(
                index, fast(own_b), *map(fast, pieces), *map(fast, halos), hbm(current), hbm(diagonal), hbm(previous),
            )

        def alpha(own_a, chunk, rounds, keep, recv, halos, rest, so_far):
            w, tile = parts[chunk], tile_of(chunk)
            here = column(own_alpha, tile, starts[chunk] // tile)
            operands = [index, *map(fast, (own_a, keep, recv, *halos, rest))]
            in_specs = [pl.BlockSpec((a_rows, slots, blk, blk), lambda g, _: (0, 0, 0, 0))]
            in_specs += [column(own_alpha, tile)] * 2
            in_specs += [column(a_halo * blk, tile)] * 2
            in_specs += [here]
            aliases = {}
            if so_far is not None:
                aliases = {len(operands): 0}
                operands.append(hbm(so_far))
                in_specs.append(free)
            out_shape = [pltpu.HBM((own_alpha, own_beta), f32)]
            out_specs = [here]
            if rounds:
                out_shape.append(shape(own_alpha, w))
                out_specs.append(column(own_alpha, tile))
            return pl.pallas_call(
                functools.partial(alpha_kernel, spots, (a_per, a_rows, a_halo, blk), rounds),
                out_shape=out_shape,
                grid_spec=pltpu.PrefetchScalarGridSpec(
                    num_scalar_prefetch=1,
                    grid=(w // tile,),
                    in_specs=in_specs,
                    out_specs=out_specs,
                    scratch_shapes=[
                        VM(((2 * a_halo + a_per + 1) * blk, tile), bf16),
                        VM((a_rows * blk, tile), bf16),
                    ],
                ),
                input_output_aliases=aliases,
                compiler_params=limit(10),
                cost_estimate=cost(2 * a_rows * slots * blk * blk * w, 16 * own_alpha * w),
                name="alpha",
            )(*operands)

        pieces = []
        for chunk in chunks:
            pieces.append(rounded(chunk))
        index = pl.pallas_call(
            functools.partial(index_kernel, (spots, slots, a_per, a_rows, a_halo, b_per, b_halo)),
            out_shape=jax.ShapeDtypeStruct((spots.size,), i32),
            in_specs=[smem] * 7,
            out_specs=smem,
            scratch_shapes=[
                SM((slots, row_blocks), i32),
                SM((slots, beta_blocks.shape[0]), i32),
                SM((2, max(a_per, b_per)), i32),
            ],
            compiler_params=limit(4),
            cost_estimate=cost(10_000_000, 1_000_000),
            name="index",
        )(at, *smem_tables)

        def weights(blocks, first, count, at_once):
            one = (at_once, slots, blk, blk)
            return pl.pallas_call(
                weights_kernel,
                out_shape=VM((count, slots, blk, blk), bf16),
                grid_spec=pltpu.PrefetchScalarGridSpec(
                    num_scalar_prefetch=1,
                    grid=(count // at_once,),
                    in_specs=[pl.BlockSpec(one, lambda g, first: (first[0] + g, 0, 0, 0))],
                    out_specs=pl.BlockSpec(one, lambda g, first: (g, 0, 0, 0)),
                ),
                compiler_params=limit(4),
                cost_estimate=cost(0, 4 * count * slots * blk * blk),
                name="weights",
            )(first, hbm(blocks))

        vectors = [prev_vector, this_vector] + [None] * STEPS
        made = {0: pieces}
        own, received, b_halos, rest, halos = {}, {}, {}, {}, {}

        def send(step, chunk):
            received[step, chunk] = lax.ppermute(made[step][chunk], "aa", swap)

        for chunk in chunks:
            send(0, chunk)
        for word in ORDER:
            kind, step, chunk = word[0], int(word[1]), int(word[2:] or 0)
            if kind == "w":
                own[step] = (
                    weights(alpha_blocks, a_first, a_rows, 1)
                    if step == 0
                    else weights(beta_blocks, b_first, b_per, b_per)
                )
            elif kind == "q":
                picked = beta_pick(made[step])
            elif kind == "p":
                picked = pick(chunk, made[step][chunk], received[step, chunk])
            elif kind == "b":
                rest[step] = beta(own[1], made[step], b_halos[step], vectors[step + 1], vectors[step])
            else:
                vectors[step + 2], *piece = alpha(
                    own[0], chunk, step < STEPS - 1, made[step][chunk], received[step, chunk],
                    halos[step, chunk], rest[step], vectors[step + 2],
                )
                made.setdefault(step + 1, []).extend(piece)
            if kind == "q":
                b_halos[step] = []
                for which in range(2):
                    b_halos[step].append(lax.ppermute(picked[which], "ba", b_ways[which]))
            if kind == "p":
                halos[step, chunk] = a_halos(picked)
            if kind == "a" and step < STEPS - 1:
                send(step + 1, chunk)
        return tuple(vectors[2:])

    if a_most <= A_MAIN and b_most <= B_MAIN:
        return body(a_most, b_most)
    further = pl.pallas_call(
        functools.partial(level_kernel, (slots, a_per, a_rows, A_MAIN, b_per, B_MAIN)),
        out_shape=jax.ShapeDtypeStruct((1,), i32),
        in_specs=[smem] * 6,
        out_specs=smem,
        scratch_shapes=[SM((slots, row_blocks), i32), SM((slots, beta_blocks.shape[0]), i32)],
        compiler_params=limit(4),
        name="level",
    )(*smem_tables)
    return lax.cond(
        further[0] != 0, lambda: body(a_most, b_most), lambda: body(min(a_most, A_MAIN), min(b_most, B_MAIN))
    )


def block_columns(class_sizes, offsets):
    class_ends = jnp.cumsum(class_sizes)
    class_starts = class_ends - class_sizes
    row_ids = jnp.arange(offsets.shape[0], dtype=jnp.int32)[:, None]
    inside = (row_ids >= class_starts[None, :]) & (row_ids < class_ends[None, :])
    first_block = jnp.sum(jnp.where(inside, class_starts[None, :], 0), axis=1)
    class_length = jnp.sum(jnp.where(inside, class_sizes[None, :], 0), axis=1)
    return first_block[:, None] + offsets % class_length[:, None]


def couple_last(pieces, blocks, columns, live_mask):
    out_blocks, _, block_size, _ = blocks.shape
    item_count = pieces.shape[0]
    stacked = pieces.reshape(item_count, -1, block_size)
    picked = stacked[:, columns, :] * live_mask[None, :, :, None]
    result = jnp.einsum("crkj,rkij->cri", picked, blocks, preferred_element_type=jnp.float32)
    return result.reshape(item_count, out_blocks * block_size).astype(jnp.bfloat16)


def whole_on_device(
    prev_vector,
    this_vector,
    diagonal,
    alpha_blocks,
    alpha_classes,
    alpha_offsets,
    alpha_mask,
    beta_blocks,
    beta_classes,
    beta_offsets,
    beta_mask,
):
    alpha_cols = block_columns(alpha_classes, alpha_offsets)
    alpha_live = alpha_mask.astype(jnp.bfloat16)
    beta_cols = block_columns(beta_classes, beta_offsets)
    beta_live = beta_mask.astype(jnp.bfloat16)
    alpha_count = lax.axis_size("aa")
    beta_count = lax.axis_size("ba")
    own_alpha, own_beta = prev_vector.shape
    own_count = beta_blocks.shape[0] // beta_count
    first_own = lax.axis_index("ba") * own_count
    own_blocks = lax.dynamic_slice_in_dim(beta_blocks, first_own, own_count, 0)
    own_cols = lax.dynamic_slice_in_dim(beta_cols, first_own, own_count, 0)
    own_live = lax.dynamic_slice_in_dim(beta_live, first_own, own_count, 0)
    previous = prev_vector
    current = this_vector
    produced = []
    for _ in range(STEPS):
        rounded = current.astype(jnp.bfloat16)
        alpha_shaped = rounded.reshape(own_alpha, alpha_count, own_beta // alpha_count)
        pieces = lax.all_to_all(alpha_shaped, "aa", split_axis=1, concat_axis=0, tiled=True)
        whole_alpha, single, columns_here = pieces.shape
        flat = pieces.reshape(whole_alpha, columns_here)
        applied = couple_last(flat.T, alpha_blocks, alpha_cols, alpha_live).T
        alpha_local = applied.reshape(whole_alpha, single, columns_here)
        alpha_back = lax.all_to_all(alpha_local, "aa", split_axis=0, concat_axis=1, tiled=True)
        alpha_term = alpha_back.reshape(own_alpha, own_beta)
        whole_rows = lax.all_gather(rounded, "ba", axis=1, tiled=True)
        beta_term = couple_last(whole_rows, own_blocks, own_cols, own_live)
        newer = (
            2.0
            * (alpha_term.astype(jnp.float32) + beta_term.astype(jnp.float32) + diagonal * current)
            - previous
        )
        previous = current
        current = newer
        produced.append(newer)
    return (produced[0], produced[-1])


def on_device(*args):
    own_alpha, own_beta = args[0].shape
    blk = args[3].shape[-1]
    fits = (
        lax.axis_size("aa") % PAIR == 0
        and (PAIR * own_alpha) % blk == 0
        and PAIR * own_alpha // blk >= A_MOST - 1
        and own_alpha % 64 == 0
        and own_beta % (sum(SHARES) * blk) == 0
        and own_beta // blk >= B_MOST - 1
        and lax.axis_size("ba") % 2 == 0
    )
    return (halo_on_device if fits else whole_on_device)(*args)


def solution(mesh):
    return jax.shard_map(
        on_device,
        mesh=mesh,
        in_specs=(P("aa", "ba"),) * 3 + (P(),) * 8,
        out_specs=(P("aa", "ba"), P("aa", "ba")),
        check_vma=False,
    )
```
